1024 devices in a mesh: lat: 32 (over z_lo, x), lon: 32 (over z_hi, y, core).
Axes of the slice: x: 8, y: 8, z: 8 (z_hi: 2, z_lo: 4; z = z_hi * 4 + z_lo), core: 2. Of those that a mesh axis runs over, the one named last changes fastest.
Arguments:
- model_state: float32 [256, 512, 960], P('lat', 'lon'), may hold values from -5 to 5
- send_slots: int32 [32, 32, 32, 4], P('lat', 'lon'), may hold values from -1 to 127, as said below
- in_weight: bfloat16 [3, 16, 406], replicated, may hold values from -0.875 to 0.875
- in_bias: float32 [406], replicated, may hold values from -4 to 4
- mid_weight: bfloat16 [406, 406], replicated, may hold values from -0.3125 to 0.3125
- mid_bias: float32 [406], replicated, may hold values from -4 to 4
- out_weight: bfloat16 [3, 406, 16], replicated, may hold values from -0.15625 to 0.15625
Outputs:
- new_state: float32 [256, 512, 960], P('lat', 'lon')
The draws below stay inside these ranges and needn't reach their ends.
Inputs may be any that keep to these rules, and one draw needn't show every extreme that they name: send_slots[a, b, d, s] is -1 for an empty slot or a local column r * 16 + c (local row r, column c) of device (a, b) that is owned for physics by the device at longitude index d of the same latitude row; no column appears twice on a device; along each latitude row of devices every owner d receives exactly 64 live entries; on some device every slot is live.
All inputs are finite; a program needn't handle non-finite values.
Results may differ from the reference program's by a relative error of at most 0.0017.
Values may be sent and summed in bfloat16 or wider, within the bound.
A program may use at most 64 MiB of HBM per device.

```python
import math
import jax
import jax.numpy as jnp
from jax import lax

CLAT = 8
CLON = 16
LEV = 60
NVAR = 16
HID = 406
SUNCAP = 128
FEAT = 960
RECV = 64
NLAT = 256
NLON = 512
N_LAT = 32
N_LON = 32


def draw_send_slots(key, part):
    column_count = CLAT * CLON
    key_shift, key_spare, key_pick = jax.random.split(jax.random.fold_in(key, 7), 3)
    subsolar = jax.random.randint(key_shift, (N_LAT, 1), 0, N_LON)
    remainder = jax.random.randint(key_spare, (N_LAT, 1), 0, SUNCAP + 1)
    lon_pos = jnp.arange(N_LON, dtype=jnp.int32)[None, :]
    phase_pos = (lon_pos - subsolar) % N_LON
    half_count = N_LON // 2
    counts = jnp.where(phase_pos < half_count, SUNCAP, 0)
    counts = jnp.where(phase_pos == 0, SUNCAP - remainder, counts)
    counts = jnp.where(phase_pos == half_count, remainder, counts)
    starts = jnp.cumsum(counts, axis=1) - counts
    scores = jax.random.randint(key_pick, (N_LAT, N_LON, column_count), 0, 65536) * column_count
    scores = scores + jnp.arange(column_count, dtype=jnp.int32)[None, None, :]
    chosen = jnp.argsort(scores, axis=-1)[..., :SUNCAP].astype(jnp.int32)
    entries = jnp.arange(SUNCAP, dtype=jnp.int32)[None, None, :]
    position = starts[..., None] + entries
    destination = position % N_LON
    first_hit = starts[..., None] + (destination - starts[..., None]) % N_LON
    slot_number = (position - first_hit) // N_LON
    per_pair = SUNCAP // N_LON
    is_valid = entries < counts[..., None]
    target = jnp.where(is_valid, destination * per_pair + slot_number, N_LON * per_pair)
    lat_index = jnp.broadcast_to(jnp.arange(N_LAT, dtype=jnp.int32)[:, None, None], target.shape)
    lon_index = jnp.broadcast_to(jnp.arange(N_LON, dtype=jnp.int32)[None, :, None], target.shape)
    slot_table = jnp.full((N_LAT, N_LON, N_LON * per_pair + 1), -1, jnp.int32)
    slot_table = slot_table.at[lat_index, lon_index, target].set(chosen)
    return slot_table[..., :N_LON * per_pair].reshape(N_LAT, N_LON, N_LON, per_pair)


def block_scale(rng, dims, cuts, low, high):
    gain, own = 1.0, jax.random.fold_in(rng, 6)
    for axis_at, blocks in cuts:
        heights = jnp.exp(jax.random.uniform(jax.random.fold_in(own, axis_at), (blocks,), jnp.float32, low / len(cuts), high / len(cuts)))
        gain = gain * jnp.repeat(heights, dims[axis_at] // blocks).reshape([-1 if axis == axis_at else 1 for axis in range(len(dims))])
    return gain


def gaussian(rng, dims, scale, most, shards=(), held_as=jnp.bfloat16):
    gain = block_scale(rng, dims, shards, -0.22, 0.18) if shards else 1.0
    values = jax.random.normal(rng, dims, jnp.float32) * scale * gain
    return jnp.minimum(jnp.maximum(values, -most), most).astype(held_as)


def setup_inputs(seed: int = 0) -> dict:
    streams_of = jax.random.split(jax.random.key(seed), 8)
    model_state = gaussian(streams_of[0], (NLAT, NLON, FEAT), 1.0, 5.0, ((0, 32), (1, 32)), jnp.float32)
    send_slots = draw_send_slots(jax.random.fold_in(streams_of[7], 71), 0)
    in_weight = gaussian(streams_of[2], (3, NVAR, HID), (3 * NVAR) ** -0.5, 0.875)
    in_bias = gaussian(streams_of[3], (HID,), 1.0, 4.0, (), jnp.float32)
    mid_weight = gaussian(streams_of[4], (HID, HID), HID ** -0.5, 0.3125)
    mid_bias = gaussian(streams_of[5], (HID,), 1.0, 4.0, (), jnp.float32)
    out_weight = gaussian(streams_of[6], (3, HID, NVAR), (3 * HID) ** -0.5, 0.15625)
    return {"model_state": model_state, "send_slots": send_slots, "in_weight": in_weight, "in_bias": in_bias, "mid_weight": mid_weight, "mid_bias": mid_bias, "out_weight": out_weight}


courant = 0.1
phys_weight = 0.5


def face_flux(lower, upper, component):
    lower_split = lower.reshape(lower.shape[:-1] + (LEV, NVAR))
    upper_split = upper.reshape(upper.shape[:-1] + (LEV, NVAR))
    speed = 0.5 * (lower_split[..., component:component + 1] + upper_split[..., component:component + 1])
    fluxes = jnp.maximum(speed, 0.0) * lower_split + jnp.minimum(speed, 0.0) * upper_split
    return fluxes.reshape(lower.shape)


def column_physics(packets, in_weight, in_bias, mid_weight, mid_bias, out_weight):
    count = packets.shape[0]
    block_size = math.gcd(count, 64)
    stacked_in = in_weight.reshape(3 * NVAR, HID)
    stacked_out = jnp.transpose(out_weight, (1, 0, 2)).reshape(HID, 3 * NVAR)

    def one_block(block_rows):
        levels = block_rows.reshape(block_size, LEV, NVAR)
        zeros_pad = jnp.zeros((block_size, 1, NVAR), levels.dtype)
        padded = jnp.concatenate([zeros_pad, levels, zeros_pad], axis=1)
        stacked = jnp.concatenate([padded[:, :-2], padded[:, 1:-1], padded[:, 2:]], axis=2)
        stacked = stacked.reshape(block_size * LEV, 3 * NVAR)
        first_hidden = jax.nn.silu(jnp.dot(stacked, stacked_in, preferred_element_type=jnp.float32) + in_bias).astype(jnp.bfloat16)
        second_hidden = jax.nn.silu(jnp.dot(first_hidden, mid_weight, preferred_element_type=jnp.float32) + mid_bias).astype(jnp.bfloat16)
        partial_value = jnp.dot(second_hidden, stacked_out, preferred_element_type=jnp.float32).reshape(block_size, LEV, 3, NVAR)
        edge = jnp.zeros((block_size, 1, NVAR), partial_value.dtype)
        from_below = jnp.concatenate([edge, partial_value[:, :-1, 0]], axis=1)
        from_above = jnp.concatenate([partial_value[:, 1:, 2], edge], axis=1)
        result = from_below + partial_value[:, :, 1] + from_above
        return result.astype(jnp.bfloat16).reshape(block_size, LEV * NVAR)

    outputs = lax.map(one_block, packets.reshape(count // block_size, block_size, LEV * NVAR))
    return outputs.reshape(count, LEV * NVAR)


def reference(model_state, send_slots, in_weight, in_bias, mid_weight, mid_bias, out_weight):
    lat_device = jnp.arange(N_LAT, dtype=jnp.int32)[:, None, None, None]
    lon_device = jnp.arange(N_LON, dtype=jnp.int32)[None, :, None, None]
    safe_slots = jnp.maximum(send_slots, 0)
    global_row = lat_device * CLAT + safe_slots // CLON
    global_col = lon_device * CLON + safe_slots % CLON
    flat_index = (global_row * NLON + global_col).reshape(-1).astype(jnp.int32)
    is_live = send_slots.reshape(-1) >= 0
    chosen = jnp.nonzero(is_live, size=N_LAT * N_LON * RECV)[0].astype(jnp.int32)
    targets = flat_index[chosen]
    columns = model_state.reshape(NLAT * NLON, FEAT)
    packets = columns[targets].astype(jnp.bfloat16)
    tendency = column_physics(packets, in_weight, in_bias, mid_weight, mid_bias, out_weight)
    physics_field = jnp.zeros((NLAT * NLON, FEAT), jnp.float32).at[targets].add(tendency.astype(jnp.float32))
    physics_field = physics_field.reshape(NLAT, NLON, FEAT)

    def one_row(row_index):
        centre = lax.dynamic_index_in_dim(model_state, row_index, 0, keepdims=False)
        southern = lax.dynamic_index_in_dim(model_state, jnp.maximum(row_index - 1, 0), 0, keepdims=False)
        southern = jnp.where(row_index > 0, southern, jnp.zeros_like(southern))
        northern = lax.dynamic_index_in_dim(model_state, jnp.minimum(row_index + 1, NLAT - 1), 0, keepdims=False)
        northern = jnp.where(row_index < NLAT - 1, northern, jnp.zeros_like(northern))
        extended = jnp.concatenate([centre[-1:], centre, centre[:1]], axis=0)
        lon_flux = face_flux(extended[:-1], extended[1:], 0)
        north_flux = face_flux(centre, northern, 1)
        south_flux = face_flux(southern, centre, 1)
        advection = -courant * ((lon_flux[1:] - lon_flux[:-1]) + (north_flux - south_flux))
        physics_row = lax.dynamic_index_in_dim(physics_field, row_index, 0, keepdims=False)
        return centre + advection + phys_weight * physics_row

    return lax.map(one_row, jnp.arange(NLAT, dtype=jnp.int32))
```

```python
import functools

import jax
import jax.numpy as jnp
from jax import lax
from jax.experimental import pallas as pl
from jax.experimental.pallas import tpu as pltpu
from jax.sharding import PartitionSpec as P

MESH = pl.DeviceIdType.MESH

LEV = 60
NVAR = 16
HID = 406
HPAD = 416
FEAT = 960
ROWS = 8
COLS = 16
CELLS = ROWS * COLS
LANES = 128
CHUNK = 4

courant = 0.1


def split3(x):
    hi = x.astype(jnp.bfloat16).astype(jnp.float32)
    mid = (x - hi).astype(jnp.bfloat16).astype(jnp.float32)
    lo = (x - hi) - mid
    return hi, mid, lo


def bias_rows(block, bias, first):
    row = lax.broadcasted_iota(jnp.int32, block.shape, 0)
    for n, part in enumerate(split3(bias)):
        block = jnp.where(row == first + n, part, block)
    return block


def swish(y):
    return (y + y * jnp.tanh(y)).astype(jnp.bfloat16)


def spread(x, component):
    lane = lax.broadcasted_iota(jnp.int32, (x.shape[0], LANES), 1)
    source = (lane // NVAR) * NVAR + component
    parts = []
    for start in range(0, FEAT, LANES):
        width = min(LANES, FEAT - start)
        part = x[:, start : start + width]
        if width < LANES:
            part = jnp.concatenate([part, jnp.zeros((x.shape[0], LANES - width), x.dtype)], axis=1)
        parts.append(jnp.take_along_axis(part, source, axis=1)[:, :width])
    return jnp.concatenate(parts, axis=1)


def flux(lower, upper, component):
    speed = spread(lower + upper, component)
    return jnp.maximum(speed, 0.0) * lower + jnp.minimum(speed, 0.0) * upper


def kernel(
    n_lat, n_lon,
    state, slots, w1, b1, wm, bm, wo, out,
    own, xt, a1, am, w1t, wmt, wot, brow, p0, p1, p2, h1, h2, result,
    edge_w, edge_e, halo_w, halo_e, halo_s, halo_n,
    load_sem, store_sem, send_sem, recv_sem,
):
    lat, lon = lax.axis_index("lat"), lax.axis_index("lon")
    east, west = lax.rem(lon + 1, n_lon), lax.rem(lon + n_lon - 1, n_lon)
    has_south, has_north = lat > 0, lat < n_lat - 1
    barrier = pltpu.get_barrier_semaphore()

    def greet(a, b):
        pl.semaphore_signal(barrier, inc=1, device_id=(a, b), device_id_type=MESH)

    greet(lat, east)
    greet(lat, west)
    pl.when(has_south)(lambda: greet(lat - 1, lon))
    pl.when(has_north)(lambda: greet(lat + 1, lon))

    load = pltpu.make_async_copy(state, own, load_sem)
    load.start()

    brow[...] = jnp.zeros_like(brow)
    brow[0:1, 0:HID] = b1[...].reshape(1, HID) * 0.5
    brow[1:2, 0:HID] = bm[...].reshape(1, HID) * 0.5
    a1[...] = jnp.zeros_like(a1)
    a1[0:48, 0:HID] = w1[...] * jnp.bfloat16(0.5)
    a1[48:64, :] = bias_rows(jnp.zeros((16, 512), jnp.float32), brow[0:1, :], 0).astype(jnp.bfloat16)
    w1t[...] = jnp.transpose(a1[...], (1, 0))
    am[...] = jnp.zeros_like(am)
    am[0:HID, 0:HID] = wm[...] * jnp.bfloat16(0.5)
    am[400:416, :] = bias_rows(am[400:416, :].astype(jnp.float32), brow[1:2, :], 6).astype(jnp.bfloat16)
    wmt[...] = jnp.transpose(am[...], (1, 0))
    wot[...] = jnp.zeros_like(wot)
    for k in range(3):
        wot[16 * k : 16 * k + 16, 0:HID] = wo[k] * jnp.bfloat16(0.5)

    load.wait()
    edge_w[...] = own[:, 0, :]
    edge_e[...] = own[:, COLS - 1, :]
    cells = own[...].reshape(CELLS, FEAT).astype(jnp.bfloat16)
    xt[0:16, :] = jnp.zeros((16, LANES), jnp.bfloat16)
    xt[16 + FEAT :, :] = jnp.zeros((16, LANES), jnp.bfloat16)
    for start in range(0, FEAT, LANES):
        width = min(LANES, FEAT - start)
        xt[16 + start : 16 + start + width, :] = jnp.transpose(cells[:, start : start + width], (1, 0))

    p0[...] = jnp.zeros_like(p0)
    p1[...] = jnp.zeros_like(p1)
    p2[...] = jnp.zeros_like(p2)
    ones = jnp.ones((16, LANES), jnp.bfloat16)
    last_row = lax.broadcasted_iota(jnp.int32, (16, CHUNK * LANES), 0)
    is_one = (last_row >= 6) & (last_row < 9)

    def physics(step, carry):
        level = step * CHUNK
        windows = []
        for j in range(CHUNK):
            start = pl.multiple_of((level + j) * 16, 16)
            windows.append(jnp.concatenate([xt[pl.ds(start, 48), :], ones], axis=0))
        window = jnp.concatenate(windows, axis=1)
        first = swish(jnp.dot(w1t[0:HPAD, :], window, preferred_element_type=jnp.float32))
        h1[0:400, :] = first[0:400]
        h1[400:416, :] = jnp.where(is_one, jnp.bfloat16(1.0), first[400:416])
        h2[...] = swish(jnp.dot(wmt[0:HPAD, 0:HPAD], h1[...], preferred_element_type=jnp.float32))
        part = jnp.dot(wot[:, 0:HPAD], h2[...], preferred_element_type=jnp.float32)
        for j in range(CHUNK):
            start = pl.multiple_of((level + j) * 16, 16)
            lanes = slice(LANES * j, LANES * (j + 1))
            p0[pl.ds(start + 32, 16), :] = part[0:16, lanes]
            p1[pl.ds(start + 16, 16), :] = part[16:32, lanes]
            p2[pl.ds(start, 16), :] = part[32:48, lanes]
        return carry

    early = 4
    lax.fori_loop(0, early, physics, 0)

    peers = 2 + has_south.astype(jnp.int32) + has_north.astype(jnp.int32)
    pl.semaphore_wait(barrier, peers)

    def copy(n, src, dst, a, b):
        return pltpu.make_async_remote_copy(
            src_ref=src, dst_ref=dst, send_sem=send_sem.at[n], recv_sem=recv_sem.at[n],
            device_id=(a, b), device_id_type=MESH,
        )

    to_east = copy(0, edge_e, halo_w, lat, east)
    to_west = copy(1, edge_w, halo_e, lat, west)
    to_north = copy(2, own.at[ROWS - 1], halo_s, lat + 1, lon)
    to_south = copy(3, own.at[0], halo_n, lat - 1, lon)
    to_east.start()
    to_west.start()
    pl.when(has_north)(lambda: to_north.start())
    pl.when(has_south)(lambda: to_south.start())

    lax.fori_loop(early, LEV // CHUNK, physics, 0)

    peers = slots.shape[1]
    column = lax.broadcasted_iota(jnp.int32, (LANES, peers), 0)
    hits = jnp.zeros((LANES, peers), jnp.float32)
    for s in range(slots.shape[0]):
        hits = jnp.where(slots[s : s + 1, :] == column, 1.0, hits)
    alive = jnp.max(hits, axis=1, keepdims=True)

    for start in range(0, FEAT, LANES):
        width = min(LANES, FEAT - start)
        rows = slice(16 + start, 16 + start + width)
        total = p0[rows, :] + p1[rows, :] + p2[rows, :]
        tend = jnp.transpose(total.astype(jnp.bfloat16), (1, 0)).astype(jnp.float32)
        tend = jnp.where(alive > 0.0, tend, 0.0)
        result[:, :, start : start + width] = own[:, :, start : start + width] + tend.reshape(
            ROWS, COLS, width
        )

    scale = -0.5 * courant
    for r in range(ROWS):
        centre = own[r]
        faces = flux(centre[:-1], centre[1:], 0)
        none = jnp.zeros((1, FEAT), jnp.float32)
        div = jnp.concatenate([faces, none], axis=0) - jnp.concatenate([none, faces], axis=0)
        result[r] = result[r] + scale * div
        if r < ROWS - 1:
            face = scale * flux(centre, own[r + 1], 1)
            result[r] = result[r] + face
            result[r + 1] = result[r + 1] - face

    pl.when(has_south)(lambda: to_north.wait_recv())
    pl.when(has_north)(lambda: to_south.wait_recv())
    south = jnp.where(has_south, halo_s[...], 0.0)
    north = jnp.where(has_north, halo_n[...], 0.0)
    result[0] = result[0] - scale * flux(south, own[0], 1)
    result[ROWS - 1] = result[ROWS - 1] + scale * flux(own[ROWS - 1], north, 1)
    to_east.wait_recv()
    to_west.wait_recv()
    result[:, 0, :] = result[:, 0, :] - scale * flux(halo_w[...], own[:, 0, :], 0)
    result[:, COLS - 1, :] = result[:, COLS - 1, :] + scale * flux(own[:, COLS - 1, :], halo_e[...], 0)

    store = pltpu.make_async_copy(result, out, store_sem)
    store.start()
    to_east.wait_send()
    to_west.wait_send()
    pl.when(has_north)(lambda: to_north.wait_send())
    pl.when(has_south)(lambda: to_south.wait_send())
    store.wait()


def shards(n_lat, n_lon, model_state, send_slots, in_weight, in_bias, mid_weight, mid_bias, out_weight):
    vmem = pl.BlockSpec(memory_space=pltpu.VMEM)
    hbm = pl.BlockSpec(memory_space=pl.ANY)
    f32, bf16 = jnp.float32, jnp.bfloat16
    return pl.pallas_call(
        functools.partial(kernel, n_lat, n_lon),
        out_shape=jax.ShapeDtypeStruct(model_state.shape, f32),
        in_specs=[hbm] + [vmem] * 6,
        out_specs=hbm,
        scratch_shapes=[
            pltpu.VMEM((ROWS, COLS, FEAT), f32),
            pltpu.VMEM((FEAT + 32, LANES), bf16),
            pltpu.VMEM((64, 512), bf16),
            pltpu.VMEM((512, 512), bf16),
            pltpu.VMEM((512, 64), bf16),
            pltpu.VMEM((512, 512), bf16),
            pltpu.VMEM((48, 512), bf16),
            pltpu.VMEM((8, 512), f32),
            pltpu.VMEM((FEAT + 32, LANES), f32),
            pltpu.VMEM((FEAT + 32, LANES), f32),
            pltpu.VMEM((FEAT + 32, LANES), f32),
            pltpu.VMEM((HPAD, CHUNK * LANES), bf16),
            pltpu.VMEM((HPAD, CHUNK * LANES), bf16),
            pltpu.VMEM((ROWS, COLS, FEAT), f32),
            pltpu.VMEM((ROWS, FEAT), f32),
            pltpu.VMEM((ROWS, FEAT), f32),
            pltpu.VMEM((ROWS, FEAT), f32),
            pltpu.VMEM((ROWS, FEAT), f32),
            pltpu.VMEM((COLS, FEAT), f32),
            pltpu.VMEM((COLS, FEAT), f32),
            pltpu.SemaphoreType.DMA,
            pltpu.SemaphoreType.DMA,
            pltpu.SemaphoreType.DMA((4,)),
            pltpu.SemaphoreType.DMA((4,)),
        ],
        compiler_params=pltpu.CompilerParams(collective_id=0, has_side_effects=True),
    )(
        model_state,
        jnp.transpose(send_slots.reshape(send_slots.shape[2:]), (1, 0)),
        in_weight.reshape(3 * NVAR, HID),
        in_bias,
        mid_weight,
        mid_bias,
        jnp.transpose(out_weight, (0, 2, 1)),
    )


def solution(mesh):
    return jax.shard_map(
        functools.partial(shards, mesh.shape["lat"], mesh.shape["lon"]),
        mesh=mesh,
        in_specs=(P("lat", "lon", None), P("lat", "lon", None, None), P(), P(), P(), P(), P()),
        out_specs=P("lat", "lon", None),
        check_vma=False,
    )
```

```python
import functools

import jax
import jax.numpy as jnp
from jax import lax
from jax.experimental import pallas as pl
from jax.experimental.pallas import tpu as pltpu
from jax.sharding import PartitionSpec as P

MESH = pl.DeviceIdType.MESH

LEV = 60
NVAR = 16
HID = 406
HPAD = 416
FEAT = 960
ROWS = 8
COLS = 16
CELLS = ROWS * COLS
LANES = 128
CHUNK = 4
VMEM_LIMIT = 66500000

courant = 0.1


def split3(x):
    hi = x.astype(jnp.bfloat16).astype(jnp.float32)
    mid = (x - hi).astype(jnp.bfloat16).astype(jnp.float32)
    lo = (x - hi) - mid
    return hi, mid, lo


def bias_rows(block, bias, first):
    row = lax.broadcasted_iota(jnp.int32, block.shape, 0)
    for n, part in enumerate(split3(bias)):
        block = jnp.where(row == first + n, part, block)
    return block


def swish(y):
    return (y + y * jnp.tanh(y)).astype(jnp.bfloat16)


def spread(x, component):
    lane = lax.broadcasted_iota(jnp.int32, (x.shape[0], LANES), 1)
    source = (lane // NVAR) * NVAR + component
    parts = []
    for start in range(0, FEAT, LANES):
        width = min(LANES, FEAT - start)
        part = x[:, start : start + width]
        if width < LANES:
            part = jnp.concatenate([part, jnp.zeros((x.shape[0], LANES - width), x.dtype)], axis=1)
        parts.append(jnp.take_along_axis(part, source, axis=1)[:, :width])
    return jnp.concatenate(parts, axis=1)


def flux(lower, upper, component):
    speed = spread(lower + upper, component)
    return jnp.maximum(speed, 0.0) * lower + jnp.minimum(speed, 0.0) * upper


EAST, WEST, NORTH, SOUTH = range(4)
OPPOSITE = (WEST, EAST, SOUTH, NORTH)


def neighbours(lat, lon, n_lat, n_lon):
    root = (lat == 0) & (lon == 0)
    half = n_lon // 2
    first_column, last_column = lon == 0, lon == n_lon - 1

    def lower_first(a):
        return (lax.rem(a, 8) < 4) | (lax.rem(a, 8) == 7)

    beside_root_e = (lat == 0) & last_column
    beside_root_w = (lat == 0) & (lon == 1)
    above_root = (lat == 1) & first_column
    has = (lon >= 0, lon >= 0, lat < n_lat - 1, lat > 0)
    first = (
        root | (last_column & (lat > 0)),
        root | ((lon > 0) & jnp.logical_not(beside_root_w)),
        root | jnp.logical_not(lower_first(lat)),
        lower_first(lat + 7) & jnp.logical_not(above_root),
    )
    far = (
        jnp.logical_not(first[EAST]) & ((lon == half - 1) | beside_root_e),
        jnp.logical_not(first[WEST]) & (first_column | beside_root_w),
        lat < 0,
        above_root,
    )
    return has, first, far


def kernel(
    n_lat, n_lon,
    state, slots_hbm, w1_hbm, b1_hbm, wm_hbm, bm_hbm, wo_hbm, out,
    own, slots, w1, b1, wm, bm, wo,
    xt, a1, am, w1t, wmt, wot, brow, p0, p1, p2, h1, h2,
    halo_e, halo_w, halo_n, halo_s,
    load_sem, send_sem, recv_sem, ready_sem,
):
    lat, lon = lax.axis_index("lat"), lax.axis_index("lon")
    has, first, far = neighbours(lat, lon, n_lat, n_lon)
    late = [jnp.logical_not(f) for f in first]
    near = [jnp.logical_not(f) for f in far]
    where = (
        (lat, lax.rem(lon + 1, n_lon)),
        (lat, lax.rem(lon + n_lon - 1, n_lon)),
        (lat + 1, lon),
        (lat - 1, lon),
    )
    barrier = pltpu.get_barrier_semaphore()

    def signal(sem, d):
        pl.semaphore_signal(sem, inc=1, device_id=where[d], device_id_type=MESH)

    for d in range(4):
        pl.when(has[d] & late[d])(functools.partial(signal, barrier, d))

    pairs = ((state, own), (w1_hbm, w1), (b1_hbm, b1), (bm_hbm, bm), (wm_hbm, wm), (wo_hbm, wo), (slots_hbm, slots))
    loads = [pltpu.make_async_copy(src, dst, load_sem.at[n]) for n, (src, dst) in enumerate(pairs)]
    for load in loads:
        load.start()

    halos = (halo_e, halo_w, halo_n, halo_s)
    edges = (state.at[:, COLS - 1, :], state.at[:, 0, :], state.at[ROWS - 1], state.at[0])
    sends = [
        pltpu.make_async_remote_copy(
            src_ref=edges[d], dst_ref=halos[OPPOSITE[d]], send_sem=send_sem.at[d], recv_sem=recv_sem.at[OPPOSITE[d]],
            device_id=where[d], device_id_type=MESH,
        )
        for d in range(4)
    ]
    count = jnp.int32(0)
    for d in range(4):
        count = count + (has[d] & first[d]).astype(jnp.int32)
    pl.when(count > 0)(lambda: pl.semaphore_wait(barrier, count))
    for d in range(4):

        @pl.when(has[d] & first[d])
        def _(d=d):
            sends[d].start()
            signal(ready_sem.at[OPPOSITE[d]], d)

    def answer(d):
        pl.semaphore_wait(ready_sem.at[d], 1)
        sends[d].start()

    a1[...] = jnp.zeros_like(a1)
    am[...] = jnp.zeros_like(am)
    wot[...] = jnp.zeros_like(wot)
    brow[...] = jnp.zeros_like(brow)
    for load in loads[1:]:
        load.wait()
    brow[0:1, 0:HID] = b1[...].reshape(1, HID) * 0.5
    brow[1:2, 0:HID] = bm[...].reshape(1, HID) * 0.5
    a1[0:48, 0:HID] = w1[...] * jnp.bfloat16(0.5)
    a1[48:64, :] = bias_rows(jnp.zeros((16, 512), jnp.float32), brow[0:1, :], 0).astype(jnp.bfloat16)
    w1t[...] = jnp.transpose(a1[...], (1, 0))
    am[0:HID, 0:HID] = wm[...] * jnp.bfloat16(0.5)
    am[400:416, :] = bias_rows(am[400:416, :].astype(jnp.float32), brow[1:2, :], 6).astype(jnp.bfloat16)
    wmt[...] = jnp.transpose(am[...], (1, 0))
    for k in range(3):
        wot[16 * k : 16 * k + 16, 0:HID] = wo[k] * jnp.bfloat16(0.5)

    loads[0].wait()
    cells = own[...].reshape(CELLS, FEAT).astype(jnp.bfloat16)
    xt[0:16, :] = jnp.zeros((16, LANES), jnp.bfloat16)
    xt[16 + FEAT :, :] = jnp.zeros((16, LANES), jnp.bfloat16)
    for start in range(0, FEAT, LANES):
        width = min(LANES, FEAT - start)
        xt[16 + start : 16 + start + width, :] = jnp.transpose(cells[:, start : start + width], (1, 0))

    p0[...] = jnp.zeros_like(p0)
    p1[...] = jnp.zeros_like(p1)
    p2[...] = jnp.zeros_like(p2)
    ones = jnp.ones((16, LANES), jnp.bfloat16)
    last_row = lax.broadcasted_iota(jnp.int32, (16, CHUNK * LANES), 0)
    is_one = (last_row >= 6) & (last_row < 9)

    def physics(step, carry):
        level = step * CHUNK
        windows = []
        for j in range(CHUNK):
            start = pl.multiple_of((level + j) * 16, 16)
            windows.append(jnp.concatenate([xt[pl.ds(start, 48), :], ones], axis=0))
        window = jnp.concatenate(windows, axis=1)
        hidden = swish(jnp.dot(w1t[0:HPAD, :], window, preferred_element_type=jnp.float32))
        h1[0:400, :] = hidden[0:400]
        h1[400:416, :] = jnp.where(is_one, jnp.bfloat16(1.0), hidden[400:416])
        h2[...] = swish(jnp.dot(wmt[0:HPAD, 0:HPAD], h1[...], preferred_element_type=jnp.float32))
        part = jnp.dot(wot[:, 0:HPAD], h2[...], preferred_element_type=jnp.float32)
        for j in range(CHUNK):
            start = pl.multiple_of((level + j) * 16, 16)
            lanes = slice(LANES * j, LANES * (j + 1))
            p0[pl.ds(start + 32, 16), :] = part[0:16, lanes]
            p1[pl.ds(start + 16, 16), :] = part[16:32, lanes]
            p2[pl.ds(start, 16), :] = part[32:48, lanes]
        return carry

    steps = LEV // CHUNK
    lax.fori_loop(0, steps // 2, physics, 0)
    for d in range(4):
        pl.when(has[d] & late[d] & near[d])(functools.partial(answer, d))
    lax.fori_loop(steps // 2, steps, physics, 0)

    peers = slots.shape[1]
    column = lax.broadcasted_iota(jnp.int32, (LANES, peers), 0)
    hits = jnp.zeros((LANES, peers), jnp.float32)
    for s in range(slots.shape[0]):
        hits = jnp.where(slots[s : s + 1, :] == column, 1.0, hits)
    alive = jnp.max(hits, axis=1, keepdims=True)

    for start in range(0, FEAT, LANES):
        width = min(LANES, FEAT - start)
        rows = slice(16 + start, 16 + start + width)
        total = p0[rows, :] + p1[rows, :] + p2[rows, :]
        tend = jnp.transpose(total.astype(jnp.bfloat16), (1, 0)).astype(jnp.float32)
        tend = jnp.where(alive > 0.0, tend, 0.0)
        out[:, :, start : start + width] = own[:, :, start : start + width] + tend.reshape(ROWS, COLS, width)

    scale = -0.5 * courant
    for r in range(ROWS):
        centre = own[r]
        faces = flux(centre[:-1], centre[1:], 0)
        none = jnp.zeros((1, FEAT), jnp.float32)
        div = jnp.concatenate([faces, none], axis=0) - jnp.concatenate([none, faces], axis=0)
        out[r] = out[r] + scale * div
        if r < ROWS - 1:
            face = scale * flux(centre, own[r + 1], 1)
            out[r] = out[r] + face
            out[r + 1] = out[r + 1] - face

    def edge(d):
        if d == EAST:
            out[:, COLS - 1, :] = out[:, COLS - 1, :] + scale * flux(own[:, COLS - 1, :], halo_e[...], 0)
        elif d == WEST:
            out[:, 0, :] = out[:, 0, :] - scale * flux(halo_w[...], own[:, 0, :], 0)
        elif d == NORTH:
            out[ROWS - 1] = out[ROWS - 1] + scale * flux(own[ROWS - 1], halo_n[...], 1)
        else:
            out[0] = out[0] - scale * flux(halo_s[...], own[0], 1)

    def outside(ref):
        ref[...] = jnp.zeros_like(ref)

    pl.when(jnp.logical_not(has[NORTH]))(functools.partial(outside, halo_n))
    pl.when(jnp.logical_not(has[SOUTH]))(functools.partial(outside, halo_s))

    def arrived(d):
        sends[OPPOSITE[d]].wait_recv()

    for d in (NORTH, SOUTH, EAST, WEST):
        pl.when(has[d] & near[d])(functools.partial(arrived, d))
        pl.when(near[d])(functools.partial(edge, d))
    for d in (SOUTH, EAST, WEST):

        @pl.when(far[d])
        def _(d=d):
            answer(d)
            arrived(d)
            edge(d)

    for d in range(4):
        pl.when(has[d])(lambda d=d: sends[d].wait_send())


def shards(n_lat, n_lon, model_state, send_slots, in_weight, in_bias, mid_weight, mid_bias, out_weight):
    f32, bf16 = jnp.float32, jnp.bfloat16
    slab = (ROWS, COLS, FEAT)
    return pl.pallas_call(
        functools.partial(kernel, n_lat, n_lon),
        out_shape=pltpu.VMEM(slab, f32),
        in_specs=[pl.BlockSpec(memory_space=pl.ANY)] * 7,
        out_specs=pl.BlockSpec(memory_space=pltpu.VMEM),
        scratch_shapes=[
            pltpu.VMEM(slab, f32),
            pltpu.VMEM((send_slots.shape[3], send_slots.shape[2]), jnp.int32),
            pltpu.VMEM((3 * NVAR, HID), bf16),
            pltpu.VMEM((HID,), f32),
            pltpu.VMEM((HID, HID), bf16),
            pltpu.VMEM((HID,), f32),
            pltpu.VMEM((3, NVAR, HID), bf16),
            pltpu.VMEM((FEAT + 32, LANES), bf16),
            pltpu.VMEM((64, 512), bf16),
            pltpu.VMEM((512, 512), bf16),
            pltpu.VMEM((512, 64), bf16),
            pltpu.VMEM((512, 512), bf16),
            pltpu.VMEM((48, 512), bf16),
            pltpu.VMEM((8, 512), f32),
            pltpu.VMEM((FEAT + 32, LANES), f32),
            pltpu.VMEM((FEAT + 32, LANES), f32),
            pltpu.VMEM((FEAT + 32, LANES), f32),
            pltpu.VMEM((HPAD, CHUNK * LANES), bf16),
            pltpu.VMEM((HPAD, CHUNK * LANES), bf16),
            pltpu.VMEM((ROWS, FEAT), f32),
            pltpu.VMEM((ROWS, FEAT), f32),
            pltpu.VMEM((COLS, FEAT), f32),
            pltpu.VMEM((COLS, FEAT), f32),
            pltpu.SemaphoreType.DMA((7,)),
            pltpu.SemaphoreType.DMA((4,)),
            pltpu.SemaphoreType.DMA((4,)),
            pltpu.SemaphoreType.REGULAR((4,)),
        ],
        compiler_params=pltpu.CompilerParams(
            collective_id=0, has_side_effects=True, vmem_limit_bytes=VMEM_LIMIT
        ),
    )(
        model_state,
        jnp.transpose(send_slots.reshape(send_slots.shape[2:]), (1, 0)),
        in_weight.reshape(3 * NVAR, HID),
        in_bias,
        mid_weight,
        mid_bias,
        jnp.transpose(out_weight, (0, 2, 1)),
    )


def solution(mesh):
    return jax.shard_map(
        functools.partial(shards, mesh.shape["lat"], mesh.shape["lon"]),
        mesh=mesh,
        in_specs=(P("lat", "lon", None), P("lat", "lon", None, None), P(), P(), P(), P(), P()),
        out_specs=P("lat", "lon", None),
        check_vma=False,
    )
```

```python
import functools

import jax
import jax.numpy as jnp
from jax import lax
from jax.experimental import pallas as pl
from jax.experimental.pallas import tpu as pltpu
from jax.sharding import PartitionSpec as P

MESH = pl.DeviceIdType.MESH

LEV = 60
NVAR = 16
HID = 406
HPAD = 416
FEAT = 960
ROWS = 8
COLS = 16
CELLS = ROWS * COLS
LANES = 128
CHUNK = 4
VMEM_LIMIT = 66500000

courant = 0.1


def split3(x):
    hi = x.astype(jnp.bfloat16).astype(jnp.float32)
    mid = (x - hi).astype(jnp.bfloat16).astype(jnp.float32)
    lo = (x - hi) - mid
    return hi, mid, lo


def bias_rows(block, bias, first):
    row = lax.broadcasted_iota(jnp.int32, block.shape, 0)
    for n, part in enumerate(split3(bias)):
        block = jnp.where(row == first + n, part, block)
    return block


def swish(y):
    return (y + y * jnp.tanh(y)).astype(jnp.bfloat16)


def spread(x, component):
    lane = lax.broadcasted_iota(jnp.int32, (x.shape[0], LANES), 1)
    source = (lane // NVAR) * NVAR + component
    parts = []
    for start in range(0, FEAT, LANES):
        width = min(LANES, FEAT - start)
        part = x[:, start : start + width]
        if width < LANES:
            part = jnp.concatenate([part, jnp.zeros((x.shape[0], LANES - width), x.dtype)], axis=1)
        parts.append(jnp.take_along_axis(part, source, axis=1)[:, :width])
    return jnp.concatenate(parts, axis=1)


def flux(lower, upper, component):
    speed = spread(lower + upper, component)
    return jnp.maximum(speed, 0.0) * lower + jnp.minimum(speed, 0.0) * upper


EAST, WEST, NORTH, SOUTH = range(4)
OPPOSITE = (WEST, EAST, SOUTH, NORTH)


def neighbours(lat, lon, n_lat, n_lon):
    root = (lat == 0) & (lon == 0)
    half = n_lon // 2
    first_column, last_column = lon == 0, lon == n_lon - 1

    def lower_first(a):
        return (lax.rem(a, 8) < 4) | (lax.rem(a, 8) == 7)

    beside_root_w = (lat == 0) & (lon == 1)
    above_root = (lat == 1) & first_column
    has = (lon >= 0, lon >= 0, lat < n_lat - 1, lat > 0)
    first = (
        root | last_column,
        (lon > 0) & jnp.logical_not(beside_root_w),
        root | jnp.logical_not(lower_first(lat)),
        lower_first(lat + 7) & jnp.logical_not(above_root),
    )
    far = (
        jnp.logical_not(first[EAST]) & (lon == half - 1),
        jnp.logical_not(first[WEST]) & ((first_column & jnp.logical_not(root)) | beside_root_w),
        lat < 0,
        above_root,
    )
    return has, first, far


def kernel(
    n_lat, n_lon,
    state, slots_hbm, w1_hbm, b1_hbm, wm_hbm, bm_hbm, wo_hbm, out,
    own, slots, w1, b1, wm, bm, wo,
    xt, a1, am, w1t, wmt, wot, brow, p0, p1, p2, h1, h2, held, sides,
    halo_e, halo_w, halo_n, halo_s,
    load_sem, send_sem, recv_sem, ready_sem, side_sem,
):
    lat, lon = lax.axis_index("lat"), lax.axis_index("lon")
    has, first, far = neighbours(lat, lon, n_lat, n_lon)
    late = [jnp.logical_not(f) for f in first]
    near = [jnp.logical_not(f) for f in far]
    where = (
        (lat, lax.rem(lon + 1, n_lon)),
        (lat, lax.rem(lon + n_lon - 1, n_lon)),
        (lat + 1, lon),
        (lat - 1, lon),
    )
    barrier = pltpu.get_barrier_semaphore()
    fetches = [
        pltpu.make_async_copy(state.at[:, c, :], sides.at[n], side_sem.at[n]) for n, c in enumerate((COLS - 1, 0))
    ]
    for fetch in fetches:
        fetch.start()

    def signal(sem, d):
        pl.semaphore_signal(sem, inc=1, device_id=where[d], device_id_type=MESH)

    for d in range(4):
        pl.when(has[d] & late[d])(functools.partial(signal, barrier, d))

    pairs = ((state, own), (w1_hbm, w1), (b1_hbm, b1), (bm_hbm, bm), (wm_hbm, wm), (wo_hbm, wo), (slots_hbm, slots))
    loads = [pltpu.make_async_copy(src, dst, load_sem.at[n]) for n, (src, dst) in enumerate(pairs)]
    halos = (halo_e, halo_w, halo_n, halo_s)
    edges = (sides.at[0], sides.at[1], state.at[ROWS - 1], state.at[0])
    sends = [
        pltpu.make_async_remote_copy(
            src_ref=edges[d], dst_ref=halos[OPPOSITE[d]], send_sem=send_sem.at[d], recv_sem=recv_sem.at[OPPOSITE[d]],
            device_id=where[d], device_id_type=MESH,
        )
        for d in range(4)
    ]
    count = jnp.int32(0)
    for d in range(4):
        count = count + (has[d] & first[d]).astype(jnp.int32)

    def enter():
        for fetch in fetches:
            fetch.wait()
        pl.when(count > 0)(lambda: pl.semaphore_wait(barrier, count))
        for d in (EAST, WEST, NORTH, SOUTH):

            @pl.when(has[d] & first[d])
            def _(d=d):
                sends[d].start()
                signal(ready_sem.at[OPPOSITE[d]], d)

    across = (lat == 0) & (lon == n_lon - 1)
    pl.when(jnp.logical_not(across))(enter)
    for load in loads:
        load.start()

    def answer(d):
        pl.semaphore_wait(ready_sem.at[d], 1)
        sends[d].start()

    a1[...] = jnp.zeros_like(a1)
    am[...] = jnp.zeros_like(am)
    wot[...] = jnp.zeros_like(wot)
    brow[...] = jnp.zeros_like(brow)
    for load in loads[1:]:
        load.wait()
    brow[0:1, 0:HID] = b1[...].reshape(1, HID) * 0.5
    brow[1:2, 0:HID] = bm[...].reshape(1, HID) * 0.5
    a1[0:48, 0:HID] = w1[...] * jnp.bfloat16(0.5)
    a1[48:64, :] = bias_rows(jnp.zeros((16, 512), jnp.float32), brow[0:1, :], 0).astype(jnp.bfloat16)
    w1t[...] = jnp.transpose(a1[...], (1, 0))
    am[0:HID, 0:HID] = wm[...] * jnp.bfloat16(0.5)
    am[400:416, :] = bias_rows(am[400:416, :].astype(jnp.float32), brow[1:2, :], 6).astype(jnp.bfloat16)
    wmt[...] = jnp.transpose(am[...], (1, 0))
    for k in range(3):
        wot[16 * k : 16 * k + 16, 0:HID] = wo[k] * jnp.bfloat16(0.5)

    loads[0].wait()
    cells = own[...].reshape(CELLS, FEAT).astype(jnp.bfloat16)
    xt[0:16, :] = jnp.zeros((16, LANES), jnp.bfloat16)
    xt[16 + FEAT :, :] = jnp.zeros((16, LANES), jnp.bfloat16)
    for start in range(0, FEAT, LANES):
        width = min(LANES, FEAT - start)
        xt[16 + start : 16 + start + width, :] = jnp.transpose(cells[:, start : start + width], (1, 0))

    p0[...] = jnp.zeros_like(p0)
    p1[...] = jnp.zeros_like(p1)
    p2[...] = jnp.zeros_like(p2)
    ones = jnp.ones((16, LANES), jnp.bfloat16)
    last_row = lax.broadcasted_iota(jnp.int32, (16, CHUNK * LANES), 0)
    is_one = (last_row >= 6) & (last_row < 9)

    def physics(step, carry):
        level = step * CHUNK
        windows = []
        for j in range(CHUNK):
            start = pl.multiple_of((level + j) * 16, 16)
            windows.append(jnp.concatenate([xt[pl.ds(start, 48), :], ones], axis=0))
        window = jnp.concatenate(windows, axis=1)
        hidden = swish(jnp.dot(w1t[0:HPAD, :], window, preferred_element_type=jnp.float32))
        h1[0:400, :] = hidden[0:400]
        h1[400:416, :] = jnp.where(is_one, jnp.bfloat16(1.0), hidden[400:416])
        h2[...] = swish(jnp.dot(wmt[0:HPAD, 0:HPAD], h1[...], preferred_element_type=jnp.float32))
        part = jnp.dot(wot[:, 0:HPAD], h2[...], preferred_element_type=jnp.float32)
        for j in range(CHUNK):
            start = pl.multiple_of((level + j) * 16, 16)
            lanes = slice(LANES * j, LANES * (j + 1))
            p0[pl.ds(start + 32, 16), :] = part[0:16, lanes]
            p1[pl.ds(start + 16, 16), :] = part[16:32, lanes]
            p2[pl.ds(start, 16), :] = part[32:48, lanes]
        return carry

    steps = LEV // CHUNK
    lax.fori_loop(0, steps // 2, physics, 0)
    pl.when(across)(enter)
    for d in range(4):
        pl.when(has[d] & late[d] & near[d])(functools.partial(answer, d))
    lax.fori_loop(steps // 2, steps, physics, 0)

    peers = slots.shape[1]
    column = lax.broadcasted_iota(jnp.int32, (LANES, peers), 0)
    hits = jnp.zeros((LANES, peers), jnp.float32)
    for s in range(slots.shape[0]):
        hits = jnp.where(slots[s : s + 1, :] == column, 1.0, hits)
    alive = jnp.max(hits, axis=1, keepdims=True)

    for start in range(0, FEAT, LANES):
        width = min(LANES, FEAT - start)
        rows = slice(16 + start, 16 + start + width)
        total = p0[rows, :] + p1[rows, :] + p2[rows, :]
        tend = jnp.transpose(total.astype(jnp.bfloat16), (1, 0)).astype(jnp.float32)
        tend = jnp.where(alive > 0.0, tend, 0.0)
        out[:, :, start : start + width] = own[:, :, start : start + width] + tend.reshape(ROWS, COLS, width)

    scale = -0.5 * courant
    for r in range(ROWS):
        centre = own[r]
        faces = flux(centre[:-1], centre[1:], 0)
        none = jnp.zeros((1, FEAT), jnp.float32)
        div = jnp.concatenate([faces, none], axis=0) - jnp.concatenate([none, faces], axis=0)
        out[r] = out[r] + scale * div
        if r < ROWS - 1:
            face = scale * flux(centre, own[r + 1], 1)
            out[r] = out[r] + face
            out[r + 1] = out[r + 1] - face

    def columns(n, c):
        held[n] = out[:, c, :]

    def edge(d):
        if d == EAST:
            out[:, COLS - 1, :] = held[0] + scale * flux(sides[0], halo_e[...], 0)
        elif d == WEST:
            out[:, 0, :] = held[1] - scale * flux(halo_w[...], sides[1], 0)
        elif d == NORTH:
            out[ROWS - 1] = out[ROWS - 1] + scale * flux(own[ROWS - 1], halo_n[...], 1)
        else:
            out[0] = out[0] - scale * flux(halo_s[...], own[0], 1)

    def outside(ref):
        ref[...] = jnp.zeros_like(ref)

    pl.when(jnp.logical_not(has[NORTH]))(functools.partial(outside, halo_n))
    pl.when(jnp.logical_not(has[SOUTH]))(functools.partial(outside, halo_s))

    def arrived(d):
        sends[OPPOSITE[d]].wait_recv()

    for d in (NORTH, SOUTH):
        pl.when(has[d] & near[d])(functools.partial(arrived, d))
        pl.when(near[d])(functools.partial(edge, d))

    @pl.when(far[SOUTH])
    def _():
        answer(SOUTH)
        arrived(SOUTH)
        edge(SOUTH)

    columns(0, COLS - 1)
    columns(1, 0)
    for d in (EAST, WEST):

        @pl.when(near[d])
        def _(d=d):
            arrived(d)
            edge(d)

    for d in (EAST, WEST):

        @pl.when(far[d])
        def _(d=d):
            pl.semaphore_wait(ready_sem.at[d], 1)
            sends[d].start()
            arrived(d)
            edge(d)

    for d in range(4):
        pl.when(has[d])(lambda d=d: sends[d].wait_send())


def shards(n_lat, n_lon, model_state, send_slots, in_weight, in_bias, mid_weight, mid_bias, out_weight):
    f32, bf16 = jnp.float32, jnp.bfloat16
    slab = (ROWS, COLS, FEAT)
    return pl.pallas_call(
        functools.partial(kernel, n_lat, n_lon),
        out_shape=pltpu.VMEM(slab, f32),
        in_specs=[pl.BlockSpec(memory_space=pl.ANY)] * 7,
        out_specs=pl.BlockSpec(memory_space=pltpu.VMEM),
        scratch_shapes=[
            pltpu.VMEM(slab, f32),
            pltpu.VMEM((send_slots.shape[3], send_slots.shape[2]), jnp.int32),
            pltpu.VMEM((3 * NVAR, HID), bf16),
            pltpu.VMEM((HID,), f32),
            pltpu.VMEM((HID, HID), bf16),
            pltpu.VMEM((HID,), f32),
            pltpu.VMEM((3, NVAR, HID), bf16),
            pltpu.VMEM((FEAT + 32, LANES), bf16),
            pltpu.VMEM((64, 512), bf16),
            pltpu.VMEM((512, 512), bf16),
            pltpu.VMEM((512, 64), bf16),
            pltpu.VMEM((512, 512), bf16),
            pltpu.VMEM((48, 512), bf16),
            pltpu.VMEM((8, 512), f32),
            pltpu.VMEM((FEAT + 32, LANES), f32),
            pltpu.VMEM((FEAT + 32, LANES), f32),
            pltpu.VMEM((FEAT + 32, LANES), f32),
            pltpu.VMEM((HPAD, CHUNK * LANES), bf16),
            pltpu.VMEM((HPAD, CHUNK * LANES), bf16),
            pltpu.VMEM((2, ROWS, FEAT), f32),
            pltpu.VMEM((2, ROWS, FEAT), f32),
            pltpu.VMEM((ROWS, FEAT), f32),
            pltpu.VMEM((ROWS, FEAT), f32),
            pltpu.VMEM((COLS, FEAT), f32),
            pltpu.VMEM((COLS, FEAT), f32),
            pltpu.SemaphoreType.DMA((7,)),
            pltpu.SemaphoreType.DMA((4,)),
            pltpu.SemaphoreType.DMA((4,)),
            pltpu.SemaphoreType.REGULAR((4,)),
            pltpu.SemaphoreType.DMA((2,)),
        ],
        compiler_params=pltpu.CompilerParams(
            collective_id=0, has_side_effects=True, vmem_limit_bytes=VMEM_LIMIT
        ),
    )(
        model_state,
        jnp.transpose(send_slots.reshape(send_slots.shape[2:]), (1, 0)),
        in_weight.reshape(3 * NVAR, HID),
        in_bias,
        mid_weight,
        mid_bias,
        jnp.transpose(out_weight, (0, 2, 1)),
    )


def solution(mesh):
    return jax.shard_map(
        functools.partial(shards, mesh.shape["lat"], mesh.shape["lon"]),
        mesh=mesh,
        in_specs=(P("lat", "lon", None), P("lat", "lon", None, None), P(), P(), P(), P(), P()),
        out_specs=P("lat", "lon", None),
        check_vma=False,
    )
```

```python
import functools

import jax
import jax.numpy as jnp
from jax import lax
from jax.experimental import pallas as pl
from jax.experimental.pallas import tpu as pltpu
from jax.sharding import PartitionSpec as P

MESH = pl.DeviceIdType.MESH

LEV = 60
NVAR = 16
HID = 406
HPAD = 416
FEAT = 960
ROWS = 8
COLS = 16
CELLS = ROWS * COLS
LANES = 128
CHUNK = 4
VMEM_LIMIT = 66500000

courant = 0.1


def split3(x):
    hi = x.astype(jnp.bfloat16).astype(jnp.float32)
    mid = (x - hi).astype(jnp.bfloat16).astype(jnp.float32)
    lo = (x - hi) - mid
    return hi, mid, lo


def bias_rows(block, bias, first):
    row = lax.broadcasted_iota(jnp.int32, block.shape, 0)
    for n, part in enumerate(split3(bias)):
        block = jnp.where(row == first + n, part, block)
    return block


def swish(y):
    return (y + y * jnp.tanh(y)).astype(jnp.bfloat16)


def spread(x, component):
    lane = lax.broadcasted_iota(jnp.int32, (x.shape[0], LANES), 1)
    source = (lane // NVAR) * NVAR + component
    parts = []
    for start in range(0, FEAT, LANES):
        width = min(LANES, FEAT - start)
        part = x[:, start : start + width]
        if width < LANES:
            part = jnp.concatenate([part, jnp.zeros((x.shape[0], LANES - width), x.dtype)], axis=1)
        parts.append(jnp.take_along_axis(part, source, axis=1)[:, :width])
    return jnp.concatenate(parts, axis=1)


def flux(lower, upper, component):
    speed = spread(lower + upper, component)
    return jnp.maximum(speed, 0.0) * lower + jnp.minimum(speed, 0.0) * upper


EAST, WEST, NORTH, SOUTH = range(4)
OPPOSITE = (WEST, EAST, SOUTH, NORTH)


def neighbours(lat, lon, n_lat, n_lon):
    root = (lat == 0) & (lon == 0)
    half = n_lon // 2
    first_column, last_column = lon == 0, lon == n_lon - 1

    def lower_first(a):
        return (lax.rem(a, 8) < 4) | (lax.rem(a, 8) == 7)

    beside_root_w = (lat == 0) & (lon == 1)
    above_root = (lat == 1) & first_column
    has = (lon >= 0, lon >= 0, lat < n_lat - 1, lat > 0)
    first = (
        root | last_column | (lon == n_lon - 2),
        (lon > 0) & jnp.logical_not(last_column | beside_root_w),
        root | jnp.logical_not(lower_first(lat)),
        lower_first(lat + 7) & jnp.logical_not(above_root),
    )
    far = (
        jnp.logical_not(first[EAST]) & (lon == half - 1),
        jnp.logical_not(first[WEST]) & ((first_column & jnp.logical_not(root)) | beside_root_w),
        lat < 0,
        above_root,
    )
    return has, first, far


def kernel(
    n_lat, n_lon,
    state, slots_hbm, w1_hbm, b1_hbm, wm_hbm, bm_hbm, wo_hbm, out,
    own, slots, w1, b1, wm, bm, wo,
    xt, a1, am, w1t, wmt, wot, brow, p0, p1, p2, h1, h2, held, sides,
    halo_e, halo_w, halo_n, halo_s,
    load_sem, send_sem, recv_sem, ready_sem, side_sem,
):
    lat, lon = lax.axis_index("lat"), lax.axis_index("lon")
    has, first, far = neighbours(lat, lon, n_lat, n_lon)
    late = [jnp.logical_not(f) for f in first]
    near = [jnp.logical_not(f) for f in far]
    where = (
        (lat, lax.rem(lon + 1, n_lon)),
        (lat, lax.rem(lon + n_lon - 1, n_lon)),
        (lat + 1, lon),
        (lat - 1, lon),
    )
    barrier = pltpu.get_barrier_semaphore()
    last_column = lon == n_lon - 1
    direct = (lon >= 0, lon >= 0, jnp.logical_not(last_column), jnp.logical_not(last_column))
    fetches = [
        pltpu.make_async_copy(state.at[:, c, :], sides.at[n], side_sem.at[n]) for n, c in enumerate((COLS - 1, 0))
    ]

    def signal(sem, d):
        pl.semaphore_signal(sem, inc=1, device_id=where[d], device_id_type=MESH)

    for d in range(4):
        pl.when(has[d] & late[d] & direct[d])(functools.partial(signal, barrier, d))

    pairs = ((state, own), (w1_hbm, w1), (b1_hbm, b1), (bm_hbm, bm), (wm_hbm, wm), (wo_hbm, wo), (slots_hbm, slots))
    loads = [pltpu.make_async_copy(src, dst, load_sem.at[n]) for n, (src, dst) in enumerate(pairs)]
    halos = (halo_e, halo_w, halo_n, halo_s)
    edges = (state.at[:, COLS - 1, :], state.at[:, 0, :], state.at[ROWS - 1], state.at[0])

    def send(d, src):
        return pltpu.make_async_remote_copy(
            src_ref=src, dst_ref=halos[OPPOSITE[d]], send_sem=send_sem.at[d], recv_sem=recv_sem.at[OPPOSITE[d]],
            device_id=where[d], device_id_type=MESH,
        )

    sends = [send(d, edges[d]) for d in range(4)]
    replies = [send(EAST, sides.at[0]), send(WEST, sides.at[1])]
    count = jnp.int32(0)
    for d in range(4):
        count = count + (has[d] & first[d] & direct[d]).astype(jnp.int32)

    def enter():
        pl.when(count > 0)(lambda: pl.semaphore_wait(barrier, count))
        for d in (EAST, WEST, NORTH, SOUTH):

            @pl.when(has[d] & first[d] & direct[d])
            def _(d=d):
                sends[d].start()
                signal(ready_sem.at[OPPOSITE[d]], d)

    across = (lat == 0) & (lon == n_lon - 1)
    pl.when(jnp.logical_not(across))(enter)
    for load in loads + fetches:
        load.start()

    def answer(d):
        pl.semaphore_wait(ready_sem.at[d], 1)
        sends[d].start()

    a1[...] = jnp.zeros_like(a1)
    am[...] = jnp.zeros_like(am)
    wot[...] = jnp.zeros_like(wot)
    brow[...] = jnp.zeros_like(brow)
    for load in loads[1:] + fetches:
        load.wait()
    brow[0:1, 0:HID] = b1[...].reshape(1, HID) * 0.5
    brow[1:2, 0:HID] = bm[...].reshape(1, HID) * 0.5
    a1[0:48, 0:HID] = w1[...] * jnp.bfloat16(0.5)
    a1[48:64, :] = bias_rows(jnp.zeros((16, 512), jnp.float32), brow[0:1, :], 0).astype(jnp.bfloat16)
    w1t[...] = jnp.transpose(a1[...], (1, 0))
    am[0:HID, 0:HID] = wm[...] * jnp.bfloat16(0.5)
    am[400:416, :] = bias_rows(am[400:416, :].astype(jnp.float32), brow[1:2, :], 6).astype(jnp.bfloat16)
    wmt[...] = jnp.transpose(am[...], (1, 0))
    for k in range(3):
        wot[16 * k : 16 * k + 16, 0:HID] = wo[k] * jnp.bfloat16(0.5)

    loads[0].wait()
    cells = own[...].reshape(CELLS, FEAT).astype(jnp.bfloat16)
    xt[0:16, :] = jnp.zeros((16, LANES), jnp.bfloat16)
    xt[16 + FEAT :, :] = jnp.zeros((16, LANES), jnp.bfloat16)
    for start in range(0, FEAT, LANES):
        width = min(LANES, FEAT - start)
        xt[16 + start : 16 + start + width, :] = jnp.transpose(cells[:, start : start + width], (1, 0))

    p0[...] = jnp.zeros_like(p0)
    p1[...] = jnp.zeros_like(p1)
    p2[...] = jnp.zeros_like(p2)
    ones = jnp.ones((16, LANES), jnp.bfloat16)
    last_row = lax.broadcasted_iota(jnp.int32, (16, CHUNK * LANES), 0)
    is_one = (last_row >= 6) & (last_row < 9)

    def physics(step, carry):
        level = step * CHUNK
        windows = []
        for j in range(CHUNK):
            start = pl.multiple_of((level + j) * 16, 16)
            windows.append(jnp.concatenate([xt[pl.ds(start, 48), :], ones], axis=0))
        window = jnp.concatenate(windows, axis=1)
        hidden = swish(jnp.dot(w1t[0:HPAD, :], window, preferred_element_type=jnp.float32))
        h1[0:400, :] = hidden[0:400]
        h1[400:416, :] = jnp.where(is_one, jnp.bfloat16(1.0), hidden[400:416])
        h2[...] = swish(jnp.dot(wmt[0:HPAD, 0:HPAD], h1[...], preferred_element_type=jnp.float32))
        part = jnp.dot(wot[:, 0:HPAD], h2[...], preferred_element_type=jnp.float32)
        for j in range(CHUNK):
            start = pl.multiple_of((level + j) * 16, 16)
            lanes = slice(LANES * j, LANES * (j + 1))
            p0[pl.ds(start + 32, 16), :] = part[0:16, lanes]
            p1[pl.ds(start + 16, 16), :] = part[16:32, lanes]
            p2[pl.ds(start, 16), :] = part[32:48, lanes]
        return carry

    steps = LEV // CHUNK
    lax.fori_loop(0, steps // 2, physics, 0)
    pl.when(across)(enter)
    for d in range(4):

        @pl.when(has[d] & late[d] & near[d] & direct[d])
        def _(d=d):
            answer(d)
            if d in (NORTH, SOUTH):
                pl.when(lon == n_lon - 2)(functools.partial(signal, ready_sem.at[d], EAST))

    for d in (NORTH, SOUTH):

        @pl.when(has[d] & late[d] & last_column)
        def _(d=d):
            answer(d)
            signal(ready_sem.at[OPPOSITE[d]], d)

    for d in (NORTH, SOUTH):
        pl.when(has[d] & first[d] & last_column)(functools.partial(answer, d))
    lax.fori_loop(steps // 2, steps, physics, 0)

    peers = slots.shape[1]
    column = lax.broadcasted_iota(jnp.int32, (LANES, peers), 0)
    hits = jnp.zeros((LANES, peers), jnp.float32)
    for s in range(slots.shape[0]):
        hits = jnp.where(slots[s : s + 1, :] == column, 1.0, hits)
    alive = jnp.max(hits, axis=1, keepdims=True)

    for start in range(0, FEAT, LANES):
        width = min(LANES, FEAT - start)
        rows = slice(16 + start, 16 + start + width)
        total = p0[rows, :] + p1[rows, :] + p2[rows, :]
        tend = jnp.transpose(total.astype(jnp.bfloat16), (1, 0)).astype(jnp.float32)
        tend = jnp.where(alive > 0.0, tend, 0.0)
        out[:, :, start : start + width] = own[:, :, start : start + width] + tend.reshape(ROWS, COLS, width)

    scale = -0.5 * courant
    for r in range(ROWS):
        centre = own[r]
        faces = flux(centre[:-1], centre[1:], 0)
        none = jnp.zeros((1, FEAT), jnp.float32)
        div = jnp.concatenate([faces, none], axis=0) - jnp.concatenate([none, faces], axis=0)
        out[r] = out[r] + scale * div
        if r < ROWS - 1:
            face = scale * flux(centre, own[r + 1], 1)
            out[r] = out[r] + face
            out[r + 1] = out[r + 1] - face

    def columns(n, c):
        held[n] = out[:, c, :]

    def edge(d):
        if d == EAST:
            out[:, COLS - 1, :] = held[0] + scale * flux(sides[0], halo_e[...], 0)
        elif d == WEST:
            out[:, 0, :] = held[1] - scale * flux(halo_w[...], sides[1], 0)
        elif d == NORTH:
            out[ROWS - 1] = out[ROWS - 1] + scale * flux(own[ROWS - 1], halo_n[...], 1)
        else:
            out[0] = out[0] - scale * flux(halo_s[...], own[0], 1)

    def outside(ref):
        ref[...] = jnp.zeros_like(ref)

    pl.when(jnp.logical_not(has[NORTH]))(functools.partial(outside, halo_n))
    pl.when(jnp.logical_not(has[SOUTH]))(functools.partial(outside, halo_s))

    def arrived(d):
        sends[OPPOSITE[d]].wait_recv()

    for d in (NORTH, SOUTH):
        pl.when(has[d] & near[d])(functools.partial(arrived, d))
        pl.when(near[d])(functools.partial(edge, d))

    @pl.when(far[SOUTH])
    def _():
        answer(SOUTH)
        arrived(SOUTH)
        edge(SOUTH)

    columns(0, COLS - 1)
    columns(1, 0)
    for d in (EAST, WEST):

        @pl.when(near[d])
        def _(d=d):
            arrived(d)
            edge(d)

    for d in (EAST, WEST):

        @pl.when(far[d])
        def _(d=d):
            pl.semaphore_wait(ready_sem.at[d], 1)
            replies[d].start()
            arrived(d)
            edge(d)

    for d in range(4):
        pl.when(has[d])(lambda d=d: sends[d].wait_send())


def shards(n_lat, n_lon, model_state, send_slots, in_weight, in_bias, mid_weight, mid_bias, out_weight):
    f32, bf16 = jnp.float32, jnp.bfloat16
    slab = (ROWS, COLS, FEAT)
    return pl.pallas_call(
        functools.partial(kernel, n_lat, n_lon),
        out_shape=pltpu.VMEM(slab, f32),
        in_specs=[pl.BlockSpec(memory_space=pl.ANY)] * 7,
        out_specs=pl.BlockSpec(memory_space=pltpu.VMEM),
        scratch_shapes=[
            pltpu.VMEM(slab, f32),
            pltpu.VMEM((send_slots.shape[3], send_slots.shape[2]), jnp.int32),
            pltpu.VMEM((3 * NVAR, HID), bf16),
            pltpu.VMEM((HID,), f32),
            pltpu.VMEM((HID, HID), bf16),
            pltpu.VMEM((HID,), f32),
            pltpu.VMEM((3, NVAR, HID), bf16),
            pltpu.VMEM((FEAT + 32, LANES), bf16),
            pltpu.VMEM((64, 512), bf16),
            pltpu.VMEM((512, 512), bf16),
            pltpu.VMEM((512, 64), bf16),
            pltpu.VMEM((512, 512), bf16),
            pltpu.VMEM((48, 512), bf16),
            pltpu.VMEM((8, 512), f32),
            pltpu.VMEM((FEAT + 32, LANES), f32),
            pltpu.VMEM((FEAT + 32, LANES), f32),
            pltpu.VMEM((FEAT + 32, LANES), f32),
            pltpu.VMEM((HPAD, CHUNK * LANES), bf16),
            pltpu.VMEM((HPAD, CHUNK * LANES), bf16),
            pltpu.VMEM((2, ROWS, FEAT), f32),
            pltpu.VMEM((2, ROWS, FEAT), f32),
            pltpu.VMEM((ROWS, FEAT), f32),
            pltpu.VMEM((ROWS, FEAT), f32),
            pltpu.VMEM((COLS, FEAT), f32),
            pltpu.VMEM((COLS, FEAT), f32),
            pltpu.SemaphoreType.DMA((7,)),
            pltpu.SemaphoreType.DMA((4,)),
            pltpu.SemaphoreType.DMA((4,)),
            pltpu.SemaphoreType.REGULAR((4,)),
            pltpu.SemaphoreType.DMA((2,)),
        ],
        compiler_params=pltpu.CompilerParams(
            collective_id=0, has_side_effects=True, vmem_limit_bytes=VMEM_LIMIT
        ),
    )(
        model_state,
        jnp.transpose(send_slots.reshape(send_slots.shape[2:]), (1, 0)),
        in_weight.reshape(3 * NVAR, HID),
        in_bias,
        mid_weight,
        mid_bias,
        jnp.transpose(out_weight, (0, 2, 1)),
    )


def solution(mesh):
    return jax.shard_map(
        functools.partial(shards, mesh.shape["lat"], mesh.shape["lon"]),
        mesh=mesh,
        in_specs=(P("lat", "lon", None), P("lat", "lon", None, None), P(), P(), P(), P(), P()),
        out_specs=P("lat", "lon", None),
        check_vma=False,
    )
```

```python
import functools

import jax
import jax.numpy as jnp
from jax import lax
from jax.experimental import pallas as pl
from jax.experimental.pallas import tpu as pltpu
from jax.sharding import PartitionSpec as P

MESH = pl.DeviceIdType.MESH

LEV = 60
NVAR = 16
HID = 406
HPAD = 416
FEAT = 960
ROWS = 8
COLS = 16
CELLS = ROWS * COLS
LANES = 128
CHUNK = 4
VMEM_LIMIT = 66500000

courant = 0.1


def split3(x):
    hi = x.astype(jnp.bfloat16).astype(jnp.float32)
    mid = (x - hi).astype(jnp.bfloat16).astype(jnp.float32)
    lo = (x - hi) - mid
    return hi, mid, lo


def bias_rows(block, bias, first):
    row = lax.broadcasted_iota(jnp.int32, block.shape, 0)
    for n, part in enumerate(split3(bias)):
        block = jnp.where(row == first + n, part, block)
    return block


def swish(y):
    return (y + y * jnp.tanh(y)).astype(jnp.bfloat16)


def spread(x, component):
    lane = lax.broadcasted_iota(jnp.int32, (x.shape[0], LANES), 1)
    source = (lane // NVAR) * NVAR + component
    parts = []
    for start in range(0, FEAT, LANES):
        width = min(LANES, FEAT - start)
        part = x[:, start : start + width]
        if width < LANES:
            part = jnp.concatenate([part, jnp.zeros((x.shape[0], LANES - width), x.dtype)], axis=1)
        parts.append(jnp.take_along_axis(part, source, axis=1)[:, :width])
    return jnp.concatenate(parts, axis=1)


def flux(lower, upper, component):
    speed = spread(lower + upper, component)
    return jnp.maximum(speed, 0.0) * lower + jnp.minimum(speed, 0.0) * upper


EAST, WEST, NORTH, SOUTH = range(4)
OPPOSITE = (WEST, EAST, SOUTH, NORTH)


def neighbours(lat, lon, n_lat, n_lon):
    root = (lat == 0) & (lon == 0)
    half = n_lon // 2
    first_column, last_column = lon == 0, lon == n_lon - 1

    def lower_first(a):
        return (lax.rem(a, 8) < 4) | (lax.rem(a, 8) == 7)

    beside_root_w = (lat == 0) & (lon == 1)
    above_root = (lat == 1) & first_column
    has = (lon >= 0, lon >= 0, lat < n_lat - 1, lat > 0)
    first = (
        root | last_column | (lon == n_lon - 2),
        (lon > 0) & jnp.logical_not(last_column | beside_root_w),
        root | jnp.logical_not(lower_first(lat)),
        lower_first(lat + 7) & jnp.logical_not(above_root),
    )
    far = (
        jnp.logical_not(first[EAST]) & (lon == half - 1),
        jnp.logical_not(first[WEST]) & ((first_column & jnp.logical_not(root)) | beside_root_w),
        lat < 0,
        above_root,
    )
    return has, first, far


def kernel(
    n_lat, n_lon,
    state, slots_hbm, w1_hbm, b1_hbm, wm_hbm, bm_hbm, wo_hbm, out,
    own, slots, w1, b1, wm, bm, wo,
    xt, a1, am, w1t, wmt, wot, brow, p0, p1, p2, h1, h2, held, sides,
    halo_e, halo_w, halo_n, halo_s,
    load_sem, send_sem, recv_sem, ready_sem, side_sem,
):
    lat, lon = lax.axis_index("lat"), lax.axis_index("lon")
    has, first, far = neighbours(lat, lon, n_lat, n_lon)
    late = [jnp.logical_not(f) for f in first]
    near = [jnp.logical_not(f) for f in far]
    where = (
        (lat, lax.rem(lon + 1, n_lon)),
        (lat, lax.rem(lon + n_lon - 1, n_lon)),
        (lat + 1, lon),
        (lat - 1, lon),
    )
    barrier = pltpu.get_barrier_semaphore()
    last_column = lon == n_lon - 1
    direct = (lon >= 0, lon >= 0, jnp.logical_not(last_column), jnp.logical_not(last_column))
    fetches = [
        pltpu.make_async_copy(state.at[:, c, :], sides.at[n], side_sem.at[n]) for n, c in enumerate((COLS - 1, 0))
    ]

    def signal(sem, d):
        pl.semaphore_signal(sem, inc=1, device_id=where[d], device_id_type=MESH)


    halos = (halo_e, halo_w, halo_n, halo_s)
    edges = (state.at[:, COLS - 1, :], state.at[:, 0, :], state.at[ROWS - 1], state.at[0])

    def send(d, src):
        return pltpu.make_async_remote_copy(
            src_ref=src, dst_ref=halos[OPPOSITE[d]], send_sem=send_sem.at[d], recv_sem=recv_sem.at[OPPOSITE[d]],
            device_id=where[d], device_id_type=MESH,
        )

    sends = [send(d, edges[d]) for d in range(4)]
    replies = [send(EAST, sides.at[0]), send(WEST, sides.at[1])]
    count = jnp.int32(0)
    for d in range(4):
        count = count + (has[d] & first[d] & direct[d]).astype(jnp.int32)

    def enter():
        pl.when(count > 0)(lambda: pl.semaphore_wait(barrier, count))
        for d in (EAST, WEST, NORTH, SOUTH):

            @pl.when(has[d] & first[d] & direct[d])
            def _(d=d):
                sends[d].start()
                signal(ready_sem.at[OPPOSITE[d]], d)

    across = (lat == 0) & (lon == n_lon - 1)
    @pl.when(last_column & jnp.logical_not(across))
    def _():
        pl.semaphore_wait(barrier, 1)
        sends[EAST].start()
        signal(ready_sem.at[WEST], EAST)

    for d in range(4):
        pl.when(has[d] & late[d] & direct[d])(functools.partial(signal, barrier, d))
    pl.when(jnp.logical_not(last_column))(enter)
    pairs = ((state, own), (w1_hbm, w1), (b1_hbm, b1), (bm_hbm, bm), (wm_hbm, wm), (wo_hbm, wo), (slots_hbm, slots))
    loads = [pltpu.make_async_copy(src, dst, load_sem.at[n]) for n, (src, dst) in enumerate(pairs)]
    for load in loads + fetches:
        load.start()

    def answer(d):
        pl.semaphore_wait(ready_sem.at[d], 1)
        sends[d].start()

    a1[...] = jnp.zeros_like(a1)
    am[...] = jnp.zeros_like(am)
    wot[...] = jnp.zeros_like(wot)
    brow[...] = jnp.zeros_like(brow)
    for load in loads[1:] + fetches:
        load.wait()
    brow[0:1, 0:HID] = b1[...].reshape(1, HID) * 0.5
    brow[1:2, 0:HID] = bm[...].reshape(1, HID) * 0.5
    a1[0:48, 0:HID] = w1[...] * jnp.bfloat16(0.5)
    a1[48:64, :] = bias_rows(jnp.zeros((16, 512), jnp.float32), brow[0:1, :], 0).astype(jnp.bfloat16)
    w1t[...] = jnp.transpose(a1[...], (1, 0))
    am[0:HID, 0:HID] = wm[...] * jnp.bfloat16(0.5)
    am[400:416, :] = bias_rows(am[400:416, :].astype(jnp.float32), brow[1:2, :], 6).astype(jnp.bfloat16)
    wmt[...] = jnp.transpose(am[...], (1, 0))
    for k in range(3):
        wot[16 * k : 16 * k + 16, 0:HID] = wo[k] * jnp.bfloat16(0.5)

    loads[0].wait()
    cells = own[...].reshape(CELLS, FEAT).astype(jnp.bfloat16)
    xt[0:16, :] = jnp.zeros((16, LANES), jnp.bfloat16)
    xt[16 + FEAT :, :] = jnp.zeros((16, LANES), jnp.bfloat16)
    for start in range(0, FEAT, LANES):
        width = min(LANES, FEAT - start)
        xt[16 + start : 16 + start + width, :] = jnp.transpose(cells[:, start : start + width], (1, 0))

    p0[...] = jnp.zeros_like(p0)
    p1[...] = jnp.zeros_like(p1)
    p2[...] = jnp.zeros_like(p2)
    ones = jnp.ones((16, LANES), jnp.bfloat16)
    last_row = lax.broadcasted_iota(jnp.int32, (16, CHUNK * LANES), 0)
    is_one = (last_row >= 6) & (last_row < 9)

    def physics(step, carry):
        level = step * CHUNK
        windows = []
        for j in range(CHUNK):
            start = pl.multiple_of((level + j) * 16, 16)
            windows.append(jnp.concatenate([xt[pl.ds(start, 48), :], ones], axis=0))
        window = jnp.concatenate(windows, axis=1)
        hidden = swish(jnp.dot(w1t[0:HPAD, :], window, preferred_element_type=jnp.float32))
        h1[0:400, :] = hidden[0:400]
        h1[400:416, :] = jnp.where(is_one, jnp.bfloat16(1.0), hidden[400:416])
        h2[...] = swish(jnp.dot(wmt[0:HPAD, 0:HPAD], h1[...], preferred_element_type=jnp.float32))
        part = jnp.dot(wot[:, 0:HPAD], h2[...], preferred_element_type=jnp.float32)
        for j in range(CHUNK):
            start = pl.multiple_of((level + j) * 16, 16)
            lanes = slice(LANES * j, LANES * (j + 1))
            p0[pl.ds(start + 32, 16), :] = part[0:16, lanes]
            p1[pl.ds(start + 16, 16), :] = part[16:32, lanes]
            p2[pl.ds(start, 16), :] = part[32:48, lanes]
        return carry

    steps = LEV // CHUNK
    lax.fori_loop(0, steps // 2, physics, 0)
    pl.when(across)(enter)
    for d in range(4):

        @pl.when(has[d] & late[d] & near[d] & direct[d])
        def _(d=d):
            answer(d)
            if d in (NORTH, SOUTH):
                pl.when(lon == n_lon - 2)(functools.partial(signal, ready_sem.at[d], EAST))

    for d in (NORTH, SOUTH):

        @pl.when(has[d] & late[d] & last_column)
        def _(d=d):
            answer(d)
            signal(ready_sem.at[OPPOSITE[d]], d)

    for d in (NORTH, SOUTH):
        pl.when(has[d] & first[d] & last_column)(functools.partial(answer, d))
    lax.fori_loop(steps // 2, steps, physics, 0)

    peers = slots.shape[1]
    column = lax.broadcasted_iota(jnp.int32, (LANES, peers), 0)
    hits = jnp.zeros((LANES, peers), jnp.float32)
    for s in range(slots.shape[0]):
        hits = jnp.where(slots[s : s + 1, :] == column, 1.0, hits)
    alive = jnp.max(hits, axis=1, keepdims=True)

    for start in range(0, FEAT, LANES):
        width = min(LANES, FEAT - start)
        rows = slice(16 + start, 16 + start + width)
        total = p0[rows, :] + p1[rows, :] + p2[rows, :]
        tend = jnp.transpose(total.astype(jnp.bfloat16), (1, 0)).astype(jnp.float32)
        tend = jnp.where(alive > 0.0, tend, 0.0)
        out[:, :, start : start + width] = own[:, :, start : start + width] + tend.reshape(ROWS, COLS, width)

    scale = -0.5 * courant
    for r in range(ROWS):
        centre = own[r]
        faces = flux(centre[:-1], centre[1:], 0)
        none = jnp.zeros((1, FEAT), jnp.float32)
        div = jnp.concatenate([faces, none], axis=0) - jnp.concatenate([none, faces], axis=0)
        out[r] = out[r] + scale * div
        if r < ROWS - 1:
            face = scale * flux(centre, own[r + 1], 1)
            out[r] = out[r] + face
            out[r + 1] = out[r + 1] - face

    def columns(n, c):
        held[n] = out[:, c, :]

    def edge(d):
        if d == EAST:
            out[:, COLS - 1, :] = held[0] + scale * flux(sides[0], halo_e[...], 0)
        elif d == WEST:
            out[:, 0, :] = held[1] - scale * flux(halo_w[...], sides[1], 0)
        elif d == NORTH:
            out[ROWS - 1] = out[ROWS - 1] + scale * flux(own[ROWS - 1], halo_n[...], 1)
        else:
            out[0] = out[0] - scale * flux(halo_s[...], own[0], 1)

    def outside(ref):
        ref[...] = jnp.zeros_like(ref)

    pl.when(jnp.logical_not(has[NORTH]))(functools.partial(outside, halo_n))
    pl.when(jnp.logical_not(has[SOUTH]))(functools.partial(outside, halo_s))

    def arrived(d):
        sends[OPPOSITE[d]].wait_recv()

    for d in (NORTH, SOUTH):
        pl.when(has[d] & near[d])(functools.partial(arrived, d))
        pl.when(near[d])(functools.partial(edge, d))

    @pl.when(far[SOUTH])
    def _():
        answer(SOUTH)
        arrived(SOUTH)
        edge(SOUTH)

    columns(0, COLS - 1)
    columns(1, 0)
    for d in (EAST, WEST):

        @pl.when(near[d])
        def _(d=d):
            arrived(d)
            edge(d)

    for d in range(4):
        pl.when(has[d] & near[d])(lambda d=d: sends[d].wait_send())
    pl.when(far[SOUTH])(lambda: sends[SOUTH].wait_send())

    for d in (EAST, WEST):

        @pl.when(far[d])
        def _(d=d):
            pl.semaphore_wait(ready_sem.at[d], 1)
            replies[d].start()
            arrived(d)
            edge(d)
            replies[d].wait_send()


def shards(n_lat, n_lon, model_state, send_slots, in_weight, in_bias, mid_weight, mid_bias, out_weight):
    f32, bf16 = jnp.float32, jnp.bfloat16
    slab = (ROWS, COLS, FEAT)
    return pl.pallas_call(
        functools.partial(kernel, n_lat, n_lon),
        out_shape=pltpu.VMEM(slab, f32),
        in_specs=[pl.BlockSpec(memory_space=pl.ANY)] * 7,
        out_specs=pl.BlockSpec(memory_space=pltpu.VMEM),
        scratch_shapes=[
            pltpu.VMEM(slab, f32),
            pltpu.VMEM((send_slots.shape[3], send_slots.shape[2]), jnp.int32),
            pltpu.VMEM((3 * NVAR, HID), bf16),
            pltpu.VMEM((HID,), f32),
            pltpu.VMEM((HID, HID), bf16),
            pltpu.VMEM((HID,), f32),
            pltpu.VMEM((3, NVAR, HID), bf16),
            pltpu.VMEM((FEAT + 32, LANES), bf16),
            pltpu.VMEM((64, 512), bf16),
            pltpu.VMEM((512, 512), bf16),
            pltpu.VMEM((512, 64), bf16),
            pltpu.VMEM((512, 512), bf16),
            pltpu.VMEM((48, 512), bf16),
            pltpu.VMEM((8, 512), f32),
            pltpu.VMEM((FEAT + 32, LANES), f32),
            pltpu.VMEM((FEAT + 32, LANES), f32),
            pltpu.VMEM((FEAT + 32, LANES), f32),
            pltpu.VMEM((HPAD, CHUNK * LANES), bf16),
            pltpu.VMEM((HPAD, CHUNK * LANES), bf16),
            pltpu.VMEM((2, ROWS, FEAT), f32),
            pltpu.VMEM((2, ROWS, FEAT), f32),
            pltpu.VMEM((ROWS, FEAT), f32),
            pltpu.VMEM((ROWS, FEAT), f32),
            pltpu.VMEM((COLS, FEAT), f32),
            pltpu.VMEM((COLS, FEAT), f32),
            pltpu.SemaphoreType.DMA((7,)),
            pltpu.SemaphoreType.DMA((4,)),
            pltpu.SemaphoreType.DMA((4,)),
            pltpu.SemaphoreType.REGULAR((4,)),
            pltpu.SemaphoreType.DMA((2,)),
        ],
        compiler_params=pltpu.CompilerParams(
            collective_id=0, has_side_effects=True, vmem_limit_bytes=VMEM_LIMIT
        ),
    )(
        model_state,
        jnp.transpose(send_slots.reshape(send_slots.shape[2:]), (1, 0)),
        in_weight.reshape(3 * NVAR, HID),
        in_bias,
        mid_weight,
        mid_bias,
        jnp.transpose(out_weight, (0, 2, 1)),
    )


def solution(mesh):
    return jax.shard_map(
        functools.partial(shards, mesh.shape["lat"], mesh.shape["lon"]),
        mesh=mesh,
        in_specs=(P("lat", "lon", None), P("lat", "lon", None, None), P(), P(), P(), P(), P()),
        out_specs=P("lat", "lon", None),
        check_vma=False,
    )
```

```python
import functools

import jax
import jax.numpy as jnp
from jax import lax
from jax.experimental import pallas as pl
from jax.experimental.pallas import tpu as pltpu
from jax.sharding import PartitionSpec as P

MESH = pl.DeviceIdType.MESH

LEV = 60
NVAR = 16
HID = 406
HPAD = 416
FEAT = 960
ROWS = 8
COLS = 16
CELLS = ROWS * COLS
LANES = 128
CHUNK = 4
VMEM_LIMIT = 66500000

courant = 0.1


def split3(x):
    hi = x.astype(jnp.bfloat16).astype(jnp.float32)
    mid = (x - hi).astype(jnp.bfloat16).astype(jnp.float32)
    lo = (x - hi) - mid
    return hi, mid, lo


def bias_rows(block, bias, first):
    row = lax.broadcasted_iota(jnp.int32, block.shape, 0)
    for n, part in enumerate(split3(bias)):
        block = jnp.where(row == first + n, part, block)
    return block


def swish(y):
    return (y + y * jnp.tanh(y)).astype(jnp.bfloat16)


def spread(x, component):
    lane = lax.broadcasted_iota(jnp.int32, (x.shape[0], LANES), 1)
    source = (lane // NVAR) * NVAR + component
    parts = []
    for start in range(0, FEAT, LANES):
        width = min(LANES, FEAT - start)
        part = x[:, start : start + width]
        if width < LANES:
            part = jnp.concatenate([part, jnp.zeros((x.shape[0], LANES - width), x.dtype)], axis=1)
        parts.append(jnp.take_along_axis(part, source, axis=1)[:, :width])
    return jnp.concatenate(parts, axis=1)


def flux(lower, upper, component):
    speed = spread(lower + upper, component)
    return jnp.maximum(speed, 0.0) * lower + jnp.minimum(speed, 0.0) * upper


EAST, WEST, NORTH, SOUTH = range(4)
OPPOSITE = (WEST, EAST, SOUTH, NORTH)


def neighbours(lat, lon, n_lat, n_lon):
    root = (lat == 0) & (lon == 0)
    half = n_lon // 2
    first_column, last_column = lon == 0, lon == n_lon - 1

    def lower_first(a):
        return (lax.rem(a, 8) < 4) | (lax.rem(a, 8) == 7)

    beside_root_w = (lat == 0) & (lon == 1)
    above_root = (lat == 1) & first_column
    has = (lon >= 0, lon >= 0, lat < n_lat - 1, lat > 0)
    first = (
        root | last_column | (lon == n_lon - 2),
        (lon > 0) & jnp.logical_not(last_column | beside_root_w),
        root | jnp.logical_not(lower_first(lat)),
        lower_first(lat + 7) & jnp.logical_not(above_root),
    )
    far = (
        jnp.logical_not(first[EAST]) & (lon == half - 1),
        jnp.logical_not(first[WEST]) & ((first_column & jnp.logical_not(root)) | beside_root_w),
        lat < 0,
        above_root,
    )
    return has, first, far


def kernel(
    n_lat, n_lon,
    state, slots_hbm, w1_hbm, b1_hbm, wm_hbm, bm_hbm, wo_hbm, out,
    own, slots, w1, b1, wm, bm, wo,
    xt, a1, am, w1t, wmt, wot, brow, p0, p1, p2, h1, h2, held, sides,
    halo_e, halo_w, halo_n, halo_s,
    load_sem, send_sem, recv_sem, ready_sem, side_sem,
):
    lat, lon = lax.axis_index("lat"), lax.axis_index("lon")
    where = (
        (lat, lax.rem(lon + 1, n_lon)),
        (lat, lax.rem(lon + n_lon - 1, n_lon)),
        (jnp.minimum(lat + 1, n_lat - 1), lon),
        (jnp.maximum(lat - 1, 0), lon),
    )
    barrier = pltpu.get_barrier_semaphore()
    last_column = lon == n_lon - 1
    fetches = [
        pltpu.make_async_copy(state.at[:, c, :], sides.at[n], side_sem.at[n]) for n, c in enumerate((COLS - 1, 0))
    ]

    def signal(sem, d):
        pl.semaphore_signal(sem, inc=1, device_id=where[d], device_id_type=MESH)

    halos = (halo_e, halo_w, halo_n, halo_s)
    edges = (state.at[:, COLS - 1, :], state.at[:, 0, :], state.at[ROWS - 1], state.at[0])

    def send(d, src):
        return pltpu.make_async_remote_copy(
            src_ref=src, dst_ref=halos[OPPOSITE[d]], send_sem=send_sem.at[d], recv_sem=recv_sem.at[OPPOSITE[d]],
            device_id=where[d], device_id_type=MESH,
        )

    sends = [send(d, edges[d]) for d in range(4)]
    replies = [send(EAST, sides.at[0]), send(WEST, sides.at[1])]
    across = (lat == 0) & last_column

    @pl.when(last_column & jnp.logical_not(across))
    def _():
        pl.semaphore_wait(barrier, 1)
        sends[EAST].start()
        signal(ready_sem.at[WEST], EAST)

    has, first, far = neighbours(lat, lon, n_lat, n_lon)
    late = [jnp.logical_not(f) for f in first]
    near = [jnp.logical_not(f) for f in far]
    direct = (lon >= 0, lon >= 0, jnp.logical_not(last_column), jnp.logical_not(last_column))
    count = jnp.int32(0)
    for d in range(4):
        count = count + (has[d] & first[d] & direct[d]).astype(jnp.int32)

    def enter():
        pl.when(count > 0)(lambda: pl.semaphore_wait(barrier, count))
        for d in (EAST, WEST, NORTH, SOUTH):

            @pl.when(has[d] & first[d] & direct[d])
            def _(d=d):
                sends[d].start()
                signal(ready_sem.at[OPPOSITE[d]], d)

    for d in range(4):
        pl.when(has[d] & late[d] & direct[d])(functools.partial(signal, barrier, d))
    pl.when(jnp.logical_not(last_column))(enter)
    pairs = ((state, own), (w1_hbm, w1), (b1_hbm, b1), (bm_hbm, bm), (wm_hbm, wm), (wo_hbm, wo), (slots_hbm, slots))
    loads = [pltpu.make_async_copy(src, dst, load_sem.at[n]) for n, (src, dst) in enumerate(pairs)]
    for load in loads + fetches:
        load.start()

    def answer(d):
        pl.semaphore_wait(ready_sem.at[d], 1)
        sends[d].start()

    a1[...] = jnp.zeros_like(a1)
    am[...] = jnp.zeros_like(am)
    wot[...] = jnp.zeros_like(wot)
    brow[...] = jnp.zeros_like(brow)
    for load in loads[1:] + fetches:
        load.wait()
    brow[0:1, 0:HID] = b1[...].reshape(1, HID) * 0.5
    brow[1:2, 0:HID] = bm[...].reshape(1, HID) * 0.5
    a1[0:48, 0:HID] = w1[...] * jnp.bfloat16(0.5)
    a1[48:64, :] = bias_rows(jnp.zeros((16, 512), jnp.float32), brow[0:1, :], 0).astype(jnp.bfloat16)
    w1t[...] = jnp.transpose(a1[...], (1, 0))
    am[0:HID, 0:HID] = wm[...] * jnp.bfloat16(0.5)
    am[400:416, :] = bias_rows(am[400:416, :].astype(jnp.float32), brow[1:2, :], 6).astype(jnp.bfloat16)
    wmt[...] = jnp.transpose(am[...], (1, 0))
    for k in range(3):
        wot[16 * k : 16 * k + 16, 0:HID] = wo[k] * jnp.bfloat16(0.5)

    loads[0].wait()
    cells = own[...].reshape(CELLS, FEAT).astype(jnp.bfloat16)
    xt[0:16, :] = jnp.zeros((16, LANES), jnp.bfloat16)
    xt[16 + FEAT :, :] = jnp.zeros((16, LANES), jnp.bfloat16)
    for start in range(0, FEAT, LANES):
        width = min(LANES, FEAT - start)
        xt[16 + start : 16 + start + width, :] = jnp.transpose(cells[:, start : start + width], (1, 0))

    p0[...] = jnp.zeros_like(p0)
    p1[...] = jnp.zeros_like(p1)
    p2[...] = jnp.zeros_like(p2)
    ones = jnp.ones((16, LANES), jnp.bfloat16)
    last_row = lax.broadcasted_iota(jnp.int32, (16, CHUNK * LANES), 0)
    is_one = (last_row >= 6) & (last_row < 9)

    def physics(step, carry):
        level = step * CHUNK
        windows = []
        for j in range(CHUNK):
            start = pl.multiple_of((level + j) * 16, 16)
            windows.append(jnp.concatenate([xt[pl.ds(start, 48), :], ones], axis=0))
        window = jnp.concatenate(windows, axis=1)
        hidden = swish(jnp.dot(w1t[0:HPAD, :], window, preferred_element_type=jnp.float32))
        h1[0:400, :] = hidden[0:400]
        h1[400:416, :] = jnp.where(is_one, jnp.bfloat16(1.0), hidden[400:416])
        h2[...] = swish(jnp.dot(wmt[0:HPAD, 0:HPAD], h1[...], preferred_element_type=jnp.float32))
        part = jnp.dot(wot[:, 0:HPAD], h2[...], preferred_element_type=jnp.float32)
        for j in range(CHUNK):
            start = pl.multiple_of((level + j) * 16, 16)
            lanes = slice(LANES * j, LANES * (j + 1))
            p0[pl.ds(start + 32, 16), :] = part[0:16, lanes]
            p1[pl.ds(start + 16, 16), :] = part[16:32, lanes]
            p2[pl.ds(start, 16), :] = part[32:48, lanes]
        return carry

    steps = LEV // CHUNK
    lax.fori_loop(0, steps // 2, physics, 0)
    pl.when(across)(enter)
    for d in range(4):

        @pl.when(has[d] & late[d] & near[d] & direct[d])
        def _(d=d):
            answer(d)
            if d in (NORTH, SOUTH):
                pl.when(lon == n_lon - 2)(functools.partial(signal, ready_sem.at[d], EAST))

    for d in (NORTH, SOUTH):

        @pl.when(has[d] & late[d] & last_column)
        def _(d=d):
            answer(d)
            signal(ready_sem.at[OPPOSITE[d]], d)

    for d in (NORTH, SOUTH):
        pl.when(has[d] & first[d] & last_column)(functools.partial(answer, d))
    lax.fori_loop(steps // 2, steps, physics, 0)

    peers = slots.shape[1]
    column = lax.broadcasted_iota(jnp.int32, (LANES, peers), 0)
    hits = jnp.zeros((LANES, peers), jnp.float32)
    for s in range(slots.shape[0]):
        hits = jnp.where(slots[s : s + 1, :] == column, 1.0, hits)
    alive = jnp.max(hits, axis=1, keepdims=True)

    for start in range(0, FEAT, LANES):
        width = min(LANES, FEAT - start)
        rows = slice(16 + start, 16 + start + width)
        total = p0[rows, :] + p1[rows, :] + p2[rows, :]
        tend = jnp.transpose(total.astype(jnp.bfloat16), (1, 0)).astype(jnp.float32)
        tend = jnp.where(alive > 0.0, tend, 0.0)
        out[:, :, start : start + width] = own[:, :, start : start + width] + tend.reshape(ROWS, COLS, width)

    scale = -0.5 * courant
    for r in range(ROWS):
        centre = own[r]
        faces = flux(centre[:-1], centre[1:], 0)
        none = jnp.zeros((1, FEAT), jnp.float32)
        div = jnp.concatenate([faces, none], axis=0) - jnp.concatenate([none, faces], axis=0)
        out[r] = out[r] + scale * div
        if r < ROWS - 1:
            face = scale * flux(centre, own[r + 1], 1)
            out[r] = out[r] + face
            out[r + 1] = out[r + 1] - face

    def columns(n, c):
        held[n] = out[:, c, :]

    def edge(d):
        if d == EAST:
            out[:, COLS - 1, :] = held[0] + scale * flux(sides[0], halo_e[...], 0)
        elif d == WEST:
            out[:, 0, :] = held[1] - scale * flux(halo_w[...], sides[1], 0)
        elif d == NORTH:
            out[ROWS - 1] = out[ROWS - 1] + scale * flux(own[ROWS - 1], halo_n[...], 1)
        else:
            out[0] = out[0] - scale * flux(halo_s[...], own[0], 1)

    def outside(ref):
        ref[...] = jnp.zeros_like(ref)

    pl.when(jnp.logical_not(has[NORTH]))(functools.partial(outside, halo_n))
    pl.when(jnp.logical_not(has[SOUTH]))(functools.partial(outside, halo_s))

    def arrived(d):
        sends[OPPOSITE[d]].wait_recv()

    for d in (NORTH, SOUTH):
        pl.when(has[d] & near[d])(functools.partial(arrived, d))
        pl.when(near[d])(functools.partial(edge, d))

    @pl.when(far[SOUTH])
    def _():
        answer(SOUTH)
        arrived(SOUTH)
        edge(SOUTH)

    columns(0, COLS - 1)
    columns(1, 0)
    for d in (EAST, WEST):

        @pl.when(near[d])
        def _(d=d):
            arrived(d)
            edge(d)

    for d in range(4):
        pl.when(has[d] & near[d])(lambda d=d: sends[d].wait_send())
    pl.when(far[SOUTH])(lambda: sends[SOUTH].wait_send())

    for d in (EAST, WEST):

        @pl.when(far[d])
        def _(d=d):
            pl.semaphore_wait(ready_sem.at[d], 1)
            replies[d].start()
            arrived(d)
            edge(d)
            replies[d].wait_send()


def shards(n_lat, n_lon, model_state, send_slots, in_weight, in_bias, mid_weight, mid_bias, out_weight):
    f32, bf16 = jnp.float32, jnp.bfloat16
    slab = (ROWS, COLS, FEAT)
    return pl.pallas_call(
        functools.partial(kernel, n_lat, n_lon),
        out_shape=pltpu.VMEM(slab, f32),
        in_specs=[pl.BlockSpec(memory_space=pl.ANY)] * 7,
        out_specs=pl.BlockSpec(memory_space=pltpu.VMEM),
        scratch_shapes=[
            pltpu.VMEM(slab, f32),
            pltpu.VMEM((send_slots.shape[3], send_slots.shape[2]), jnp.int32),
            pltpu.VMEM((3 * NVAR, HID), bf16),
            pltpu.VMEM((HID,), f32),
            pltpu.VMEM((HID, HID), bf16),
            pltpu.VMEM((HID,), f32),
            pltpu.VMEM((3, NVAR, HID), bf16),
            pltpu.VMEM((FEAT + 32, LANES), bf16),
            pltpu.VMEM((64, 512), bf16),
            pltpu.VMEM((512, 512), bf16),
            pltpu.VMEM((512, 64), bf16),
            pltpu.VMEM((512, 512), bf16),
            pltpu.VMEM((48, 512), bf16),
            pltpu.VMEM((8, 512), f32),
            pltpu.VMEM((FEAT + 32, LANES), f32),
            pltpu.VMEM((FEAT + 32, LANES), f32),
            pltpu.VMEM((FEAT + 32, LANES), f32),
            pltpu.VMEM((HPAD, CHUNK * LANES), bf16),
            pltpu.VMEM((HPAD, CHUNK * LANES), bf16),
            pltpu.VMEM((2, ROWS, FEAT), f32),
            pltpu.VMEM((2, ROWS, FEAT), f32),
            pltpu.VMEM((ROWS, FEAT), f32),
            pltpu.VMEM((ROWS, FEAT), f32),
            pltpu.VMEM((COLS, FEAT), f32),
            pltpu.VMEM((COLS, FEAT), f32),
            pltpu.SemaphoreType.DMA((7,)),
            pltpu.SemaphoreType.DMA((4,)),
            pltpu.SemaphoreType.DMA((4,)),
            pltpu.SemaphoreType.REGULAR((4,)),
            pltpu.SemaphoreType.DMA((2,)),
        ],
        compiler_params=pltpu.CompilerParams(
            collective_id=0, has_side_effects=True, vmem_limit_bytes=VMEM_LIMIT
        ),
    )(
        model_state,
        jnp.transpose(send_slots.reshape(send_slots.shape[2:]), (1, 0)),
        in_weight.reshape(3 * NVAR, HID),
        in_bias,
        mid_weight,
        mid_bias,
        jnp.transpose(out_weight, (0, 2, 1)),
    )


def solution(mesh):
    return jax.shard_map(
        functools.partial(shards, mesh.shape["lat"], mesh.shape["lon"]),
        mesh=mesh,
        in_specs=(P("lat", "lon", None), P("lat", "lon", None, None), P(), P(), P(), P(), P()),
        out_specs=P("lat", "lon", None),
        check_vma=False,
    )
```

```python
import functools

import jax
import jax.numpy as jnp
from jax import lax
from jax.experimental import pallas as pl
from jax.experimental.pallas import tpu as pltpu
from jax.sharding import PartitionSpec as P

MESH = pl.DeviceIdType.MESH

LEV = 60
NVAR = 16
HID = 406
HPAD = 416
FEAT = 960
ROWS = 8
COLS = 16
CELLS = ROWS * COLS
LANES = 128
CHUNK = 4
VMEM_LIMIT = 66500000

courant = 0.1


def split3(x):
    hi = x.astype(jnp.bfloat16).astype(jnp.float32)
    mid = (x - hi).astype(jnp.bfloat16).astype(jnp.float32)
    lo = (x - hi) - mid
    return hi, mid, lo


def bias_rows(block, bias, first):
    row = lax.broadcasted_iota(jnp.int32, block.shape, 0)
    for n, part in enumerate(split3(bias)):
        block = jnp.where(row == first + n, part, block)
    return block


def swish(y):
    return (y + y * jnp.tanh(y)).astype(jnp.bfloat16)


def spread(x, component):
    lane = lax.broadcasted_iota(jnp.int32, (x.shape[0], LANES), 1)
    source = (lane // NVAR) * NVAR + component
    parts = []
    for start in range(0, FEAT, LANES):
        width = min(LANES, FEAT - start)
        part = x[:, start : start + width]
        if width < LANES:
            part = jnp.concatenate([part, jnp.zeros((x.shape[0], LANES - width), x.dtype)], axis=1)
        parts.append(jnp.take_along_axis(part, source, axis=1)[:, :width])
    return jnp.concatenate(parts, axis=1)


def flux(lower, upper, component):
    speed = spread(lower + upper, component)
    return jnp.maximum(speed, 0.0) * lower + jnp.minimum(speed, 0.0) * upper


EAST, WEST, NORTH, SOUTH = range(4)
OPPOSITE = (WEST, EAST, SOUTH, NORTH)


def neighbours(lat, lon, n_lat, n_lon):
    root = (lat == 0) & (lon == 0)
    half = n_lon // 2
    first_column, last_column = lon == 0, lon == n_lon - 1

    def lower_first(a):
        return (lax.rem(a, 8) < 4) | (lax.rem(a, 8) == 7)

    beside_root_w = (lat == 0) & (lon == 1)
    above_root = (lat == 1) & first_column
    has = (lon >= 0, lon >= 0, lat < n_lat - 1, lat > 0)
    first = (
        root | last_column | (lon == n_lon - 2),
        (lon > 0) & jnp.logical_not(last_column | beside_root_w),
        root | jnp.logical_not(lower_first(lat)),
        lower_first(lat + 7) & jnp.logical_not(above_root),
    )
    far = (
        jnp.logical_not(first[EAST]) & (lon == half - 1),
        jnp.logical_not(first[WEST]) & ((first_column & jnp.logical_not(root)) | beside_root_w),
        lat < 0,
        above_root,
    )
    return has, first, far


def kernel(
    n_lat, n_lon,
    state, slots_hbm, w1_hbm, b1_hbm, wm_hbm, bm_hbm, wo_hbm, out,
    own, slots, w1, b1, wm, bm, wo,
    xt, a1, am, w1t, wmt, wot, brow, p0, p1, p2, h1, h2, held, sides,
    halo_e, halo_w, halo_n, halo_s,
    load_sem, send_sem, recv_sem, ready_sem, side_sem,
):
    lat, lon = lax.axis_index("lat"), lax.axis_index("lon")
    where = (
        (lat, lax.rem(lon + 1, n_lon)),
        (lat, lax.rem(lon + n_lon - 1, n_lon)),
        (jnp.minimum(lat + 1, n_lat - 1), lon),
        (jnp.maximum(lat - 1, 0), lon),
    )
    barrier = pltpu.get_barrier_semaphore()
    last_column = lon == n_lon - 1
    fetches = [
        pltpu.make_async_copy(state.at[:, c, :], sides.at[n], side_sem.at[n]) for n, c in enumerate((COLS - 1, 0))
    ]

    def signal(sem, d):
        pl.semaphore_signal(sem, inc=1, device_id=where[d], device_id_type=MESH)

    halos = (halo_e, halo_w, halo_n, halo_s)
    edges = (state.at[:, COLS - 1, :], state.at[:, 0, :], state.at[ROWS - 1], state.at[0])

    def send(d, src):
        return pltpu.make_async_remote_copy(
            src_ref=src, dst_ref=halos[OPPOSITE[d]], send_sem=send_sem.at[d], recv_sem=recv_sem.at[OPPOSITE[d]],
            device_id=where[d], device_id_type=MESH,
        )

    sends = [send(d, edges[d]) for d in range(4)]
    replies = [send(EAST, sides.at[0]), send(WEST, sides.at[1])]
    across = (lat == 0) & last_column

    @pl.when(last_column & jnp.logical_not(across))
    def _():
        pl.semaphore_wait(barrier, 1)
        sends[EAST].start()
        signal(ready_sem.at[WEST], EAST)

    has, first, far = neighbours(lat, lon, n_lat, n_lon)
    late = [jnp.logical_not(f) for f in first]
    near = [jnp.logical_not(f) for f in far]
    direct = (lon >= 0, lon >= 0, jnp.logical_not(last_column), jnp.logical_not(last_column))
    count = jnp.int32(0)
    for d in range(4):
        count = count + (has[d] & first[d] & direct[d]).astype(jnp.int32)

    def enter():
        pl.when(count > 0)(lambda: pl.semaphore_wait(barrier, count))
        for d in (EAST, WEST, NORTH, SOUTH):

            @pl.when(has[d] & first[d] & direct[d])
            def _(d=d):
                sends[d].start()
                signal(ready_sem.at[OPPOSITE[d]], d)

    for d in range(4):
        pl.when(has[d] & late[d] & direct[d])(functools.partial(signal, barrier, d))
    pl.when(jnp.logical_not(last_column))(enter)
    pairs = ((state, own), (w1_hbm, w1), (b1_hbm, b1), (bm_hbm, bm), (wm_hbm, wm), (wo_hbm, wo), (slots_hbm, slots))
    loads = [pltpu.make_async_copy(src, dst, load_sem.at[n]) for n, (src, dst) in enumerate(pairs)]

    def answer(d):
        pl.semaphore_wait(ready_sem.at[d], 1)
        sends[d].start()

    a1[...] = jnp.zeros_like(a1)
    am[...] = jnp.zeros_like(am)
    wot[...] = jnp.zeros_like(wot)
    brow[...] = jnp.zeros_like(brow)
    p0[...] = jnp.zeros_like(p0)
    p1[...] = jnp.zeros_like(p1)
    p2[...] = jnp.zeros_like(p2)
    for load in loads + fetches:
        load.start()
    for load in loads[1:] + fetches:
        load.wait()
    brow[0:1, 0:HID] = b1[...].reshape(1, HID) * 0.5
    brow[1:2, 0:HID] = bm[...].reshape(1, HID) * 0.5
    a1[0:48, 0:HID] = w1[...] * jnp.bfloat16(0.5)
    a1[48:64, :] = bias_rows(jnp.zeros((16, 512), jnp.float32), brow[0:1, :], 0).astype(jnp.bfloat16)
    w1t[...] = jnp.transpose(a1[...], (1, 0))
    am[0:HID, 0:HID] = wm[...] * jnp.bfloat16(0.5)
    am[400:416, :] = bias_rows(am[400:416, :].astype(jnp.float32), brow[1:2, :], 6).astype(jnp.bfloat16)
    wmt[...] = jnp.transpose(am[...], (1, 0))
    for k in range(3):
        wot[16 * k : 16 * k + 16, 0:HID] = wo[k] * jnp.bfloat16(0.5)

    loads[0].wait()
    cells = own[...].reshape(CELLS, FEAT).astype(jnp.bfloat16)
    xt[0:16, :] = jnp.zeros((16, LANES), jnp.bfloat16)
    xt[16 + FEAT :, :] = jnp.zeros((16, LANES), jnp.bfloat16)
    for start in range(0, FEAT, LANES):
        width = min(LANES, FEAT - start)
        xt[16 + start : 16 + start + width, :] = jnp.transpose(cells[:, start : start + width], (1, 0))

    ones = jnp.ones((16, LANES), jnp.bfloat16)
    last_row = lax.broadcasted_iota(jnp.int32, (16, CHUNK * LANES), 0)
    is_one = (last_row >= 6) & (last_row < 9)

    def physics(step, carry):
        level = step * CHUNK
        windows = []
        for j in range(CHUNK):
            start = pl.multiple_of((level + j) * 16, 16)
            windows.append(jnp.concatenate([xt[pl.ds(start, 48), :], ones], axis=0))
        window = jnp.concatenate(windows, axis=1)
        hidden = swish(jnp.dot(w1t[0:HPAD, :], window, preferred_element_type=jnp.float32))
        h1[0:400, :] = hidden[0:400]
        h1[400:416, :] = jnp.where(is_one, jnp.bfloat16(1.0), hidden[400:416])
        h2[...] = swish(jnp.dot(wmt[0:HPAD, 0:HPAD], h1[...], preferred_element_type=jnp.float32))
        part = jnp.dot(wot[:, 0:HPAD], h2[...], preferred_element_type=jnp.float32)
        for j in range(CHUNK):
            start = pl.multiple_of((level + j) * 16, 16)
            lanes = slice(LANES * j, LANES * (j + 1))
            p0[pl.ds(start + 32, 16), :] = part[0:16, lanes]
            p1[pl.ds(start + 16, 16), :] = part[16:32, lanes]
            p2[pl.ds(start, 16), :] = part[32:48, lanes]
        return carry

    steps = LEV // CHUNK
    lax.fori_loop(0, steps // 2, physics, 0)
    pl.when(across)(enter)
    for d in range(4):

        @pl.when(has[d] & late[d] & near[d] & direct[d])
        def _(d=d):
            answer(d)
            if d in (NORTH, SOUTH):
                pl.when(lon == n_lon - 2)(functools.partial(signal, ready_sem.at[d], EAST))

    for d in (NORTH, SOUTH):

        @pl.when(has[d] & late[d] & last_column)
        def _(d=d):
            answer(d)
            signal(ready_sem.at[OPPOSITE[d]], d)

    for d in (NORTH, SOUTH):
        pl.when(has[d] & first[d] & last_column)(functools.partial(answer, d))
    lax.fori_loop(steps // 2, steps, physics, 0)

    peers = slots.shape[1]
    column = lax.broadcasted_iota(jnp.int32, (LANES, peers), 0)
    hits = jnp.zeros((LANES, peers), jnp.float32)
    for s in range(slots.shape[0]):
        hits = jnp.where(slots[s : s + 1, :] == column, 1.0, hits)
    alive = jnp.max(hits, axis=1, keepdims=True)

    for start in range(0, FEAT, LANES):
        width = min(LANES, FEAT - start)
        rows = slice(16 + start, 16 + start + width)
        total = p0[rows, :] + p1[rows, :] + p2[rows, :]
        tend = jnp.transpose(total.astype(jnp.bfloat16), (1, 0)).astype(jnp.float32)
        tend = jnp.where(alive > 0.0, tend, 0.0)
        out[:, :, start : start + width] = own[:, :, start : start + width] + tend.reshape(ROWS, COLS, width)

    scale = -0.5 * courant
    for r in range(ROWS):
        centre = own[r]
        faces = flux(centre[:-1], centre[1:], 0)
        none = jnp.zeros((1, FEAT), jnp.float32)
        div = jnp.concatenate([faces, none], axis=0) - jnp.concatenate([none, faces], axis=0)
        out[r] = out[r] + scale * div
        if r < ROWS - 1:
            face = scale * flux(centre, own[r + 1], 1)
            out[r] = out[r] + face
            out[r + 1] = out[r + 1] - face

    def columns(n, c):
        held[n] = out[:, c, :]

    def edge(d):
        if d == EAST:
            out[:, COLS - 1, :] = held[0] + scale * flux(sides[0], halo_e[...], 0)
        elif d == WEST:
            out[:, 0, :] = held[1] - scale * flux(halo_w[...], sides[1], 0)
        elif d == NORTH:
            out[ROWS - 1] = out[ROWS - 1] + scale * flux(own[ROWS - 1], halo_n[...], 1)
        else:
            out[0] = out[0] - scale * flux(halo_s[...], own[0], 1)

    def outside(ref):
        ref[...] = jnp.zeros_like(ref)

    pl.when(jnp.logical_not(has[NORTH]))(functools.partial(outside, halo_n))
    pl.when(jnp.logical_not(has[SOUTH]))(functools.partial(outside, halo_s))

    def arrived(d):
        sends[OPPOSITE[d]].wait_recv()

    for d in (NORTH, SOUTH):
        pl.when(has[d] & near[d])(functools.partial(arrived, d))
        pl.when(near[d])(functools.partial(edge, d))

    @pl.when(far[SOUTH])
    def _():
        answer(SOUTH)
        arrived(SOUTH)
        edge(SOUTH)

    columns(0, COLS - 1)
    columns(1, 0)
    for d in (EAST, WEST):

        @pl.when(near[d])
        def _(d=d):
            arrived(d)
            edge(d)

    for d in range(4):
        pl.when(has[d] & near[d])(lambda d=d: sends[d].wait_send())
    pl.when(far[SOUTH])(lambda: sends[SOUTH].wait_send())

    for d in (EAST, WEST):

        @pl.when(far[d])
        def _(d=d):
            pl.semaphore_wait(ready_sem.at[d], 1)
            replies[d].start()
            arrived(d)
            edge(d)
            replies[d].wait_send()


def shards(n_lat, n_lon, model_state, send_slots, in_weight, in_bias, mid_weight, mid_bias, out_weight):
    f32, bf16 = jnp.float32, jnp.bfloat16
    slab = (ROWS, COLS, FEAT)
    return pl.pallas_call(
        functools.partial(kernel, n_lat, n_lon),
        out_shape=pltpu.VMEM(slab, f32),
        in_specs=[pl.BlockSpec(memory_space=pl.ANY)] * 7,
        out_specs=pl.BlockSpec(memory_space=pltpu.VMEM),
        scratch_shapes=[
            pltpu.VMEM(slab, f32),
            pltpu.VMEM((send_slots.shape[3], send_slots.shape[2]), jnp.int32),
            pltpu.VMEM((3 * NVAR, HID), bf16),
            pltpu.VMEM((HID,), f32),
            pltpu.VMEM((HID, HID), bf16),
            pltpu.VMEM((HID,), f32),
            pltpu.VMEM((3, NVAR, HID), bf16),
            pltpu.VMEM((FEAT + 32, LANES), bf16),
            pltpu.VMEM((64, 512), bf16),
            pltpu.VMEM((512, 512), bf16),
            pltpu.VMEM((512, 64), bf16),
            pltpu.VMEM((512, 512), bf16),
            pltpu.VMEM((48, 512), bf16),
            pltpu.VMEM((8, 512), f32),
            pltpu.VMEM((FEAT + 32, LANES), f32),
            pltpu.VMEM((FEAT + 32, LANES), f32),
            pltpu.VMEM((FEAT + 32, LANES), f32),
            pltpu.VMEM((HPAD, CHUNK * LANES), bf16),
            pltpu.VMEM((HPAD, CHUNK * LANES), bf16),
            pltpu.VMEM((2, ROWS, FEAT), f32),
            pltpu.VMEM((2, ROWS, FEAT), f32),
            pltpu.VMEM((ROWS, FEAT), f32),
            pltpu.VMEM((ROWS, FEAT), f32),
            pltpu.VMEM((COLS, FEAT), f32),
            pltpu.VMEM((COLS, FEAT), f32),
            pltpu.SemaphoreType.DMA((7,)),
            pltpu.SemaphoreType.DMA((4,)),
            pltpu.SemaphoreType.DMA((4,)),
            pltpu.SemaphoreType.REGULAR((4,)),
            pltpu.SemaphoreType.DMA((2,)),
        ],
        compiler_params=pltpu.CompilerParams(
            collective_id=0, has_side_effects=True, vmem_limit_bytes=VMEM_LIMIT
        ),
    )(
        model_state,
        jnp.transpose(send_slots.reshape(send_slots.shape[2:]), (1, 0)),
        in_weight.reshape(3 * NVAR, HID),
        in_bias,
        mid_weight,
        mid_bias,
        jnp.transpose(out_weight, (0, 2, 1)),
    )


def solution(mesh):
    return jax.shard_map(
        functools.partial(shards, mesh.shape["lat"], mesh.shape["lon"]),
        mesh=mesh,
        in_specs=(P("lat", "lon", None), P("lat", "lon", None, None), P(), P(), P(), P(), P()),
        out_specs=P("lat", "lon", None),
        check_vma=False,
    )
```
